32 devices in a mesh: groups: 2 (over y), tile: 4 (over z), pass: 2 (over x), row: 2 (over core).
Axes of the slice: x: 2, y: 2, z: 4, core: 2. Of those that a mesh axis runs over, the one named last changes fastest.
Arguments:
- revisits: bfloat16 [32, 8, 64, 1024], P(('groups', 'pass'), ('tile', 'row')), parts along dimension 0, may hold values from -6 to 6
- shifts: int32 [32, 2], P(('groups', 'pass')), parts along dimension 0, may hold values from -32 to 32, as said below
- flags: int32 [32, 8], P('groups', ('tile', 'row')), parts along dimension 0, may hold values from 0 to 1, as said below
- norm1_gain: float32 [64], replicated, may hold values from 0.1 to 1.9
- w_query: bfloat16 [64, 64], replicated, may hold values from -0.75 to 0.75
- w_key: bfloat16 [64, 64], replicated, may hold values from -0.75 to 0.75
- w_value: bfloat16 [64, 64], replicated, may hold values from -0.75 to 0.75
- query_gain: float32 [64], replicated, may hold values from 0.1 to 1.9
- key_gain: float32 [64], replicated, may hold values from 0.1 to 1.9
- w_out: bfloat16 [64, 64], replicated, may hold values from -0.75 to 0.75
- norm2_gain: float32 [64], replicated, may hold values from 0.1 to 1.9
- w_in: bfloat16 [64, 128], replicated, may hold values from -0.75 to 0.75
- w_back: bfloat16 [128, 64], replicated, may hold values from -0.5 to 0.5
- conv_first: bfloat16 [3, 3, 64, 64], replicated, may hold values from -0.75 to 0.75
- conv_second: bfloat16 [3, 3, 64, 9], replicated, may hold values from -0.25 to 0.25
Outputs:
- output: float32 [16, 9, 1024], P(('groups', 'pass'), None, ('tile', 'row')), parts along dimension 0
The draws below stay inside these ranges and needn't reach their ends.
There are 2 independent parts, one for each index of `groups`. The reference program is written for one: setup_inputs(seed, part) draws one part's arguments, and reference() takes and returns one part's arrays. A program takes and returns all parts, laid end to end along the dimension named above; an argument that names none is the same for every part. Nothing has to cross between parts.
Inputs may be any that keep to these rules, and one draw needn't show every extreme that they name: `shifts`: some revisit has row shift 32, some -32, some column shift 32 and some -32. `flags`: every row band has at least one cloud-free revisit.
All inputs are finite; a program needn't handle non-finite values.
Results may differ from the reference program's by a relative error of at most 0.007.
Values may be sent and summed in bfloat16 or wider, within the bound.
A program may use at most 128 MiB of HBM per device.

```python
import math
import jax
import jax.numpy as jnp
from jax import lax

R = 16
C = 64
HEADS = 4
MLP = 128
OUT = 9
BR = 128
NBANDS = 8
NCOLS = 8
NROWS = 1024


def draw_shifts(key, part):
    first, second = jax.random.split(jax.random.fold_in(key, 11))
    values = jax.random.randint(first, (R, 2), -32, 33)
    picks = jax.random.permutation(second, R)
    values = values.at[picks[0], 0].set(32)
    values = values.at[picks[1], 0].set(-32)
    values = values.at[picks[2], 1].set(32)
    values = values.at[picks[3], 1].set(-32)
    return values.astype(jnp.int32)


def draw_flags(key, part):
    first, second = jax.random.split(jax.random.fold_in(key, 23))
    coins = jax.random.randint(first, (R, NBANDS), 0, 10) < 7
    keeper = jax.random.randint(second, (NBANDS,), 0, R)
    forced = jnp.arange(R)[:, None] == keeper[None, :]
    return (coins | forced).astype(jnp.int32)


def block_levels(key, shape, cuts, smallest, top_value):
    level, own = 1.0, jax.random.fold_in(key, 6)
    for dim, blocks in cuts:
        steps = jnp.exp(jax.random.uniform(jax.random.fold_in(own, dim), (blocks,), jnp.float32, smallest / len(cuts), top_value / len(cuts)))
        level = level * jnp.repeat(steps, shape[dim] // blocks).reshape([-1 if axis == dim else 1 for axis in range(len(shape))])
    return level


def bell_draw(rng, dims, spread, most, shards=(), held_as=jnp.bfloat16):
    level = block_levels(rng, dims, shards, -0.22, 0.18) if shards else 1.0
    array = jax.random.normal(rng, dims, jnp.float32) * spread * level
    return jnp.minimum(jnp.maximum(array, -most), most).astype(held_as)


def setup_inputs(seed: int = 0, part: int = 0) -> dict:
    seeds = jax.random.split(jax.random.key(seed), 16)
    own_keys = jax.random.split(jax.random.fold_in(seeds[15], part), 16)
    return {
        "revisits": bell_draw(own_keys[0], (R, NCOLS, C, NROWS), 1.0, 6.0, ((0, 2), (1, 8))),
        "shifts": draw_shifts(jax.random.fold_in(jax.random.fold_in(seeds[15], part), 71), part),
        "flags": draw_flags(jax.random.fold_in(jax.random.fold_in(seeds[15], part), 71), part),
        "norm1_gain": jnp.clip(1.0 + 0.18 * jax.random.normal(seeds[3], (C,), jnp.float32), 0.1, 1.9),
        "w_query": bell_draw(seeds[4], (C, C), C ** -0.5, 0.75),
        "w_key": bell_draw(seeds[5], (C, C), C ** -0.5, 0.75),
        "w_value": bell_draw(seeds[6], (C, C), C ** -0.5, 0.75),
        "query_gain": jnp.clip(1.0 + 0.18 * jax.random.normal(seeds[7], (C,), jnp.float32), 0.1, 1.9),
        "key_gain": jnp.clip(1.0 + 0.18 * jax.random.normal(seeds[8], (C,), jnp.float32), 0.1, 1.9),
        "w_out": bell_draw(seeds[9], (C, C), C ** -0.5, 0.75),
        "norm2_gain": jnp.clip(1.0 + 0.18 * jax.random.normal(seeds[10], (C,), jnp.float32), 0.1, 1.9),
        "w_in": bell_draw(seeds[11], (C, MLP), C ** -0.5, 0.75),
        "w_back": bell_draw(seeds[12], (MLP, C), MLP ** -0.5, 0.5),
        "conv_first": bell_draw(seeds[13], (3, 3, C, C), C ** -0.5, 0.75),
        "conv_second": bell_draw(seeds[14], (3, 3, C, OUT), (9 * C) ** -0.5, 0.25),
    }


eps = 1e-05
reach = 32

def rounded(values):
    return lax.optimization_barrier(values.astype(jnp.bfloat16)).astype(jnp.float32)

def rms_scale(values, gain):
    mean = lax.optimization_barrier(jnp.mean(values * values, axis=-2, keepdims=True))
    return values * lax.rsqrt(mean + eps) * gain[:, None]

def join_cells(cells_in, mask, norm1_gain, w_query, w_key, w_value, query_gain, key_gain, w_out, norm2_gain, w_in, w_back):
    f32 = jnp.float32
    count, width, chans, rows = cells_in.shape
    cells = cells_in.astype(f32)
    normed = rounded(rms_scale(cells, norm1_gain))
    query = jnp.einsum('rjcy,cd->rjdy', normed, w_query.astype(f32))
    keys = jnp.einsum('rjcy,cd->rjdy', normed, w_key.astype(f32))
    values = rounded(jnp.einsum('rjcy,cd->rjdy', normed, w_value.astype(f32)))
    q_hat = rounded(rms_scale(query, query_gain))
    k_hat = rounded(rms_scale(keys, key_gain))
    head_size = chans // HEADS
    q_heads = q_hat.reshape(count, width, HEADS, head_size, rows)
    k_heads = k_hat.reshape(count, width, HEADS, head_size, rows)
    v_heads = values.reshape(count, width, HEADS, head_size, rows)
    scores = jnp.einsum('rjhey,sjhey->hrsjy', q_heads, k_heads) * (1.0 / math.sqrt(head_size))
    weights = jnp.exp(scores) * mask[None, None, :, None, None]
    probs = rounded(weights / lax.optimization_barrier(jnp.sum(weights, axis=2, keepdims=True)))
    mixed = rounded(jnp.einsum('hrsjy,sjhey->rjhey', probs, v_heads)).reshape(count, width, chans, rows)
    hidden = cells + jnp.einsum('rjcy,cd->rjdy', mixed, w_out.astype(f32))
    normed_two = rounded(rms_scale(hidden, norm2_gain))
    inner = rounded(jax.nn.gelu(jnp.einsum('rjcy,cm->rjmy', normed_two, w_in.astype(f32)), approximate=True))
    tokens = hidden + jnp.einsum('rjmy,mc->rjcy', inner, w_back.astype(f32))
    total = lax.optimization_barrier(jnp.sum(tokens * mask[:, None, None, None], axis=0))
    return (total / jnp.sum(mask)).astype(jnp.bfloat16)

def convolve(values, weights):
    cols = values.shape[0]
    rows = values.shape[2]
    wide = jnp.pad(values.astype(jnp.float32), ((1, 1), (0, 0), (1, 1)))
    total = jnp.zeros((cols, weights.shape[3], rows), jnp.float32)
    for across in range(3):
        for down in range(3):
            total = total + jnp.einsum('xcy,co->xoy', wide[across:across + cols, :, down:down + rows], weights[across, down].astype(jnp.float32))
    return total

def reference(revisits, shifts, flags, norm1_gain, w_query, w_key, w_value, query_gain, key_gain, w_out, norm2_gain, w_in, w_back, conv_first, conv_second):
    padded = jnp.pad(revisits, ((0, 0), (reach, reach), (0, 0), (reach, reach)))

    def band_join(index):
        slab = lax.dynamic_slice_in_dim(padded, index * BR, BR + 2 * reach, 3)

        def single(entry, offset):
            return lax.dynamic_slice(entry, (reach + offset[1], jnp.int32(0), reach + offset[0]), (NCOLS, C, BR))
        aligned = jax.vmap(single)(slab, shifts)
        mask = lax.dynamic_slice_in_dim(flags, index, 1, 1)[:, 0].astype(jnp.float32)
        return join_cells(aligned, mask, norm1_gain, w_query, w_key, w_value, query_gain, key_gain, w_out, norm2_gain, w_in, w_back)
    bands = lax.map(band_join, jnp.arange(NBANDS, dtype=jnp.int32))
    joined = jnp.transpose(bands, (1, 2, 0, 3)).reshape(NCOLS, C, NROWS)
    act = jax.nn.gelu(convolve(joined, conv_first), approximate=True).astype(jnp.bfloat16)
    return convolve(act, conv_second)
```

```python
import functools
import math

import jax
import jax.numpy as jnp
import numpy as np
from jax import lax
from jax.experimental import pallas as pl
from jax.experimental.pallas import tpu as pltpu
from jax.sharding import PartitionSpec as P

HEADS = 4
eps = 1e-05
f32 = jnp.float32
half = jnp.bfloat16
MESH = pl.DeviceIdType.MESH
MIB = 1024 * 1024
BATCH = 8
QUERIES = 4


def whole(space=pltpu.VMEM):
    return pl.BlockSpec(memory_space=space)


def dot(weights, values):
    return jnp.dot(weights, values, preferred_element_type=f32)


def inside(col, ncols):
    return (col >= 0) & (col < ncols)


def align_kernel(
    sizes,
    shifts,
    x_ref,
    w_query,
    w_key,
    w_value,
    w_out,
    w_in,
    w1,
    w2,
    gain1,
    gain_q,
    gain_k,
    gain2,
    o_ref,
    table,
    tier,
    t_qkv,
    t_out,
    t_in,
    t_w1,
    t_w2,
    t_gains,
    foreign,
    picks,
    send,
    recv,
):
    nrow, bands, passes, groups = sizes
    _, own_cols, per, chans, rows = o_ref.shape
    ncols = own_cols * bands
    g = lax.axis_index("groups")
    p = lax.axis_index("pass")
    b = lax.axis_index("tile") * nrow + lax.axis_index("row")
    peers = [(dg, dp) for dg in range(groups) for dp in range(passes) if (dg, dp) != (0, 0)]

    def peer_id(dg, dp):
        return {"groups": (g + dg) % groups, "pass": (p + dp) % passes}

    barrier = pltpu.get_barrier_semaphore()
    for peer in peers:
        pl.semaphore_signal(barrier, inc=1, device_id=peer_id(*peer), device_id_type=MESH)

    offs = [shifts[1, r] for r in range(per)]
    lanes = lax.broadcasted_iota(jnp.int32, (1, table.shape[2]), 1)
    for r in range(per):
        col = lanes + offs[r]
        slot = jnp.zeros_like(lanes)
        for q in range(r):
            slot = slot + inside(col - offs[q], ncols).astype(jnp.int32)
        live = inside(col, ncols) & (lanes < ncols)
        table[p, r : r + 1, :] = jnp.where(live, slot * ncols + col, -1)

    for c in range(own_cols):
        rank = jnp.int32(0)
        chosen = [jnp.int32(0)] * per
        for r in range(per):
            live = inside(b * own_cols + c - offs[r], ncols).astype(jnp.int32)
            for k in range(r + 1):
                chosen[k] = chosen[k] + r * live * (rank == k).astype(jnp.int32)
            rank = rank + live
        for k in range(per):
            picks[c * per + k] = chosen[k]

    for i, ref in enumerate((w_query, w_key, w_value)):
        t_qkv[i * chans : (i + 1) * chans, :] = ref[...].T
    t_out[...] = w_out[...].T
    t_in[...] = w_in[...].T
    t_w1[...] = w1[...].T
    for i, ref in enumerate((gain1, gain_q, gain_k, gain2)):
        t_gains[i] = jnp.broadcast_to(ref[...], (rows, chans)).T
    t_w2[...] = w2[...]

    if peers:
        pl.semaphore_wait(barrier, len(peers))
    pending = []
    for n, (dg, dp) in enumerate(peers):
        target = table.at[p] if dg == 0 else foreign.at[(groups - dg) % groups - 1, p]
        copy = pltpu.make_async_remote_copy(
            src_ref=table.at[p],
            dst_ref=target,
            send_sem=send.at[n],
            recv_sem=recv.at[n],
            device_id=peer_id(dg, dp),
            device_id_type=MESH,
        )
        copy.start()
        pending.append(copy)

    lane = lax.broadcasted_iota(jnp.int32, (chans, rows), 1)
    for c in range(own_cols):

        def one(k, carry):
            r = picks[c * per + k]
            offset = shifts[0, r]
            amount = lax.rem(2 * rows - offset, rows)
            pos = lane + offset
            rolled = [
                pltpu.roll(x_ref[r, c, :, t * rows : (t + 1) * rows].astype(f32), amount, 1)
                for t in range(bands)
            ]
            zero = jnp.zeros((chans, rows), f32)
            for t in range(bands):
                low = rolled[t - 1] if t else zero
                high = rolled[t + 1] if t + 1 < bands else zero
                out = jnp.where(pos < 0, low, jnp.where(pos >= rows, high, rolled[t]))
                o_ref[t, c, k] = out.astype(half)
            return carry

        lax.fori_loop(0, per, one, 0)

    for copy in pending:
        copy.wait()
    most = jnp.max(table[...])
    if groups > 1:
        most = jnp.maximum(most, jnp.max(foreign[...]))
    tier[0] = jnp.maximum(lax.div(most, ncols), 0)


def gather_kernel(sizes, slots, s_ref, o_ref, loc, send1, recv1, send2, recv2):
    nrow, bands, passes, _ = sizes
    p = lax.axis_index("pass")
    b = lax.axis_index("tile") * nrow + lax.axis_index("row")

    def band_id(k):
        return {"tile": k // nrow, "row": k % nrow}

    barrier = pltpu.get_barrier_semaphore()
    for k in range(1, bands):
        pl.semaphore_signal(
            barrier, inc=1, device_id=band_id((b + k) % bands), device_id_type=MESH
        )
    for k in range(1, passes):
        pl.semaphore_signal(
            barrier, inc=1, device_id={"pass": (p + k) % passes}, device_id_type=MESH
        )
    own = pltpu.make_async_copy(s_ref.at[b, :, pl.ds(0, slots)], o_ref.at[p, b], loc)
    own.start()
    pl.semaphore_wait(barrier, bands + passes - 2)
    pending = []

    def forward(src, slot, index):
        for k in range(1, passes):
            copy = pltpu.make_async_remote_copy(
                src_ref=src,
                dst_ref=o_ref.at[p, index],
                send_sem=send2.at[k - 1, slot],
                recv_sem=recv2.at[k - 1, slot],
                device_id={"pass": (p + k) % passes},
                device_id_type=MESH,
            )
            copy.start()
            pending.append(copy)

    forward(s_ref.at[b, :, pl.ds(0, slots)], 0, b)
    first = []
    order = [k for k in range(1, bands)]
    order.sort(key=lambda k: min(k, bands - k))
    for k in reversed(order):
        peer = (b + k) % bands
        copy = pltpu.make_async_remote_copy(
            src_ref=s_ref.at[peer, :, pl.ds(0, slots)],
            dst_ref=o_ref.at[p, b],
            send_sem=send1.at[k - 1],
            recv_sem=recv1.at[k - 1],
            device_id=band_id(peer),
            device_id_type=MESH,
        )
        copy.start()
        first.append((k, copy))
    for k, copy in first:
        copy.wait_recv()
        source = (b + bands - k) % bands
        forward(o_ref.at[p, source], k, source)
    for _, copy in first:
        copy.wait_send()
    for copy in pending:
        copy.wait()
    own.wait()


def rms(values, gain):
    mean = jnp.mean(values * values, axis=0, keepdims=True)
    return values * lax.rsqrt(mean + eps) * gain


def join_kernel(
    cols,
    ncols,
    slots,
    table,
    flags,
    x_ref,
    gains,
    w_qkv,
    w_out,
    w_in,
    w_back,
    o_ref,
    q_s,
    k_s,
    v_s,
    mixed_s,
    total_s,
    tokens,
    starts,
    lives,
    dead,
    counts,
):
    passes, per, _ = table.shape
    _, chans, rows = x_ref.shape
    count = passes * per
    head = chans // HEADS
    scale = 1.0 / math.sqrt(head)
    stride = pl.next_power_of_2(cols + 1)
    base = lax.axis_index("pass") * cols
    at = jnp.int32(0)
    for x in range(cols):
        first = at
        zeros = jnp.int32(0)
        for r in range(count):
            code = table[r // per, r % per, base + x]
            flag = flags[0, r]
            place = (r // per * ncols + lax.rem(code, ncols)) * slots + lax.div(code, ncols)
            tokens[at] = (place + 1) * stride + x
            live = flag * (code >= 0).astype(jnp.int32)
            at = at + live
            zeros = zeros + flag - live
        tokens[at] = x
        starts[x] = first
        lives[x] = at - first
        dead[x] = zeros.astype(f32)
        counts[x] = zeros.astype(f32)
        flag_sum = (at - first + zeros).astype(f32)
        at = at + 1
    for i in range(BATCH):
        tokens[at + i] = cols
    starts[cols] = 0
    lives[cols] = 0
    dead[cols] = jnp.float32(0)
    counts[cols] = jnp.float32(1)
    batches = lax.div(at + BATCH - 1, BATCH)

    def cell_of(t):
        place = lax.div(tokens[t], stride) - 1
        return jnp.where(place >= 0, x_ref[jnp.maximum(place, 0)].astype(f32), 0.0)

    def part(values, i):
        return values[:, i * rows : (i + 1) * rows]

    def project(j, carry):
        g1, gq, gk = gains[0], gains[1], gains[2]
        normed = [rms(cell_of(j * BATCH + i), g1).astype(half) for i in range(BATCH)]
        qkv = dot(w_qkv[...], jnp.concatenate(normed, axis=1))
        for i in range(BATCH):
            one = part(qkv, i)
            t = j * BATCH + i
            q_s[t] = rms(one[:chans], gq).astype(half).astype(f32) * scale
            k_s[t] = rms(one[chans : 2 * chans], gk).astype(half).astype(f32)
            v_s[t] = one[2 * chans :].astype(half).astype(f32)
        return carry

    lax.fori_loop(0, batches, project, 0)
    total_s[...] = jnp.zeros_like(total_s)

    def attend(j, carry):
        for i0 in range(0, BATCH, QUERIES):
            owner = [lax.rem(tokens[j * BATCH + i0 + i], stride) for i in range(QUERIES)]
            begin = [starts[x] for x in owner]
            size = [lives[x] for x in owner]
            longest = functools.reduce(jnp.maximum, size)

            def keys_of(k, sums):
                out = []
                for i in range(QUERIES):
                    above, below = sums[i]
                    at = begin[i] + jnp.maximum(jnp.minimum(k, size[i] - 1), 0)
                    prod = (q_s[j * BATCH + i0 + i] * k_s[at]).reshape(HEADS, head, rows)
                    weight = jnp.exp(jnp.sum(prod, axis=1, keepdims=True))
                    weight = weight * jnp.where(k < size[i], 1.0, 0.0)
                    value = v_s[at].reshape(HEADS, head, rows)
                    out.append((above + weight * value, below + weight))
                return tuple(out)

            init = tuple(
                (
                    jnp.zeros((HEADS, head, rows), f32),
                    jnp.full((HEADS, 1, rows), counts[owner[i]], f32),
                )
                for i in range(QUERIES)
            )
            sums = lax.fori_loop(0, longest, keys_of, init)
            for i in range(QUERIES):
                above, below = sums[i]
                mixed = (above * (1.0 / below)).reshape(chans, rows).astype(half)
                mixed_s[:, (i0 + i) * rows : (i0 + i + 1) * rows] = mixed
        back = dot(w_out[...], mixed_s[...])
        g2 = gains[3]
        hidden = [cell_of(j * BATCH + i) + part(back, i) for i in range(BATCH)]
        normed = [rms(one, g2).astype(half) for one in hidden]
        inner = jax.nn.gelu(dot(w_in[...], jnp.concatenate(normed, axis=1)), approximate=True)
        added = dot(w_back[...], inner.astype(half))
        for i in range(BATCH):
            token = tokens[j * BATCH + i]
            x = lax.rem(token, stride)
            weight = jnp.where(token >= stride, 1.0, dead[x])
            total_s[x] += (hidden[i] + part(added, i)) * weight
        return carry

    lax.fori_loop(0, batches, attend, 0)
    for x in range(cols):
        o_ref[x] = (total_s[x] / flag_sum).astype(half)


MOVES = [(dp, db) for dp in (-1, 0, 1) for db in (-1, 0, 1) if (dp, db) != (0, 0)]


def decode_kernel(sizes, j_ref, w1, w2, o_ref, *scratch):
    nrow, bands, passes = sizes
    bufs = scratch[: len(MOVES)]
    taps, acts, send, recv = scratch[len(MOVES) :]
    cols, chans, rows = j_ref.shape
    p = lax.axis_index("pass")
    b = lax.axis_index("tile") * nrow + lax.axis_index("row")

    def exists(dp, db):
        ok = jnp.bool_(True)
        if dp:
            ok = ok & (p + dp >= 0) & (p + dp < passes)
        if db:
            ok = ok & (b + db >= 0) & (b + db < bands)
        return ok

    def target(dp, db):
        k = b + db
        return {"pass": p + dp, "tile": k // nrow, "row": k % nrow}

    barrier = pltpu.get_barrier_semaphore()
    neighbours = jnp.int32(0)
    for dp, db in MOVES:
        there = exists(dp, db)
        neighbours = neighbours + there.astype(jnp.int32)

        @pl.when(there)
        def _():
            pl.semaphore_signal(barrier, inc=1, device_id=target(dp, db), device_id_type=MESH)

    pl.semaphore_wait(barrier, neighbours)

    def copy_of(n):
        dp, db = MOVES[n]
        src = j_ref
        if dp:
            src = j_ref.at[pl.ds(cols - 2 if dp > 0 else 0, 2)]
        return pltpu.make_async_remote_copy(
            src_ref=src,
            dst_ref=bufs[n],
            send_sem=send.at[n],
            recv_sem=recv.at[n],
            device_id=target(dp, db),
            device_id_type=MESH,
        )

    for n, (dp, db) in enumerate(MOVES):

        @pl.when(exists(dp, db))
        def _():
            copy_of(n).start()

    for n, (dp, db) in enumerate(MOVES):

        @pl.when(exists(-dp, -db))
        def _():
            copy_of(n).wait_recv()

        @pl.when(jnp.logical_not(exists(-dp, -db)))
        def _():
            bufs[n][...] = jnp.zeros_like(bufs[n])

    def side(dp, db):
        return bufs[MOVES.index((-dp, -db))]

    lane = lax.broadcasted_iota(jnp.int32, (chans, rows), 1)
    wide_lane = lax.broadcasted_iota(jnp.int32, (chans, 2 * rows), 1)

    def widen(values):
        last = 2 * rows - 1
        return jnp.concatenate(
            [
                pltpu.roll(values, 1, 1).astype(half),
                values.astype(half),
                pltpu.roll(values, last, 1).astype(half),
            ],
            axis=0,
        )

    for n in range(cols + 4):
        dp = -1 if n < 2 else (1 if n >= cols + 2 else 0)
        at = n if dp < 0 else (n - cols - 2 if dp > 0 else n - 2)
        middle = j_ref[at] if dp == 0 else side(dp, 0)[at]
        border = jnp.where(
            lane < rows // 2, side(dp, 1)[at].astype(f32), side(dp, -1)[at].astype(f32)
        )
        taps[n] = widen(jnp.concatenate([middle.astype(f32), border], axis=1))
    row_pos = b * rows + jnp.where(wide_lane < rows + rows // 2, wide_lane, wide_lane - 2 * rows)
    row_inside = (row_pos >= 0) & (row_pos < bands * rows)
    for n in range(cols + 2):
        near = taps[n : n + 3].reshape(9 * chans, 2 * rows)
        act = jax.nn.gelu(dot(w1[...], near), approximate=True)
        col_pos = p * cols + n - 1
        inside = row_inside & (col_pos >= 0) & (col_pos < passes * cols)
        acts[n] = widen(jnp.where(inside, act, 0.0))
    for n in range(cols):
        near = acts[n : n + 3, :, :rows].reshape(9 * chans, rows)
        o_ref[n] = dot(w2[...], near)

    for n, (dp, db) in enumerate(MOVES):

        @pl.when(exists(dp, db))
        def _():
            copy_of(n).wait_send()


def local(
    sizes,
    revisits,
    shifts,
    flags,
    norm1_gain,
    w_query,
    w_key,
    w_value,
    query_gain,
    key_gain,
    w_out,
    norm2_gain,
    w_in,
    w_back,
    conv_first,
    conv_second,
):
    nrow, bands, passes, groups = sizes
    per, own_cols, chans, all_rows = revisits.shape
    rows = all_rows // bands
    ncols = own_cols * bands
    cols = ncols // passes
    count = per * passes
    outs = conv_second.shape[3]
    hidden = w_in.shape[1]
    dma = pltpu.SemaphoreType.DMA
    peers = max(groups * passes - 1, 1)
    shape = jax.ShapeDtypeStruct
    outputs = (
        shape((bands, own_cols, per, chans, rows), half),
        shape((passes, per, 128), jnp.int32),
        shape((1,), jnp.int32),
        shape((3 * chans, chans), half),
        shape((chans, chans), half),
        shape((hidden, chans), half),
        shape((chans, 9 * chans), half),
        shape((outs, 9 * chans), half),
        shape((4, chans, rows), f32),
    )
    packed, table, tier, t_qkv, t_out, t_in, t_w1, t_w2, gains = pl.pallas_call(
        functools.partial(align_kernel, sizes),
        out_shape=outputs,
        in_specs=[whole(pltpu.SMEM)] + [whole()] * 12,
        out_specs=tuple(whole(pltpu.SMEM) if n == 2 else whole() for n in range(len(outputs))),
        scratch_shapes=[
            pltpu.VMEM((max(groups - 1, 1), passes, per, 128), jnp.int32),
            pltpu.SMEM((own_cols * per,), jnp.int32),
            dma((peers,)),
            dma((peers,)),
        ],
        compiler_params=pltpu.CompilerParams(
            collective_id=0, has_side_effects=True, vmem_limit_bytes=16 * MIB
        ),
        name="align",
    )(
        shifts.T,
        revisits,
        w_query,
        w_key,
        w_value,
        w_out,
        w_in,
        conv_first.reshape(9 * chans, -1),
        conv_second.transpose(3, 0, 1, 2).reshape(outs, 9 * chans),
        *(gain.reshape(1, chans) for gain in (norm1_gain, query_gain, key_gain, norm2_gain)),
    )
    others = max(passes - 1, 1)
    most = cols * (count + 1)
    room = (most + BATCH - 1) // BATCH * BATCH
    w_back_t = w_back.T

    def branch(slots):
        def run(packed, table, flags, gains, t_qkv, t_out, t_in, w_back_t):
            banded = pl.pallas_call(
                functools.partial(gather_kernel, sizes, slots),
                out_shape=shape((passes, bands, own_cols, slots, chans, rows), half),
                in_specs=[whole(pl.ANY)],
                out_specs=whole(),
                scratch_shapes=[
                    dma,
                    dma((bands,)),
                    dma((bands,)),
                    dma((others, bands)),
                    dma((others, bands)),
                ],
                compiler_params=pltpu.CompilerParams(
                    collective_id=2 + slots, has_side_effects=True, vmem_limit_bytes=16 * MIB
                ),
                name="exchange",
            )(packed)
            return pl.pallas_call(
                functools.partial(join_kernel, cols, ncols, slots),
                out_shape=shape((cols, chans, rows), half),
                in_specs=[whole(pltpu.SMEM), whole(pltpu.SMEM)] + [whole()] * 6,
                out_specs=whole(),
                scratch_shapes=[
                    pltpu.VMEM((room, chans, rows), f32),
                    pltpu.VMEM((room, chans, rows), f32),
                    pltpu.VMEM((room, chans, rows), f32),
                    pltpu.VMEM((chans, BATCH * rows), half),
                    pltpu.VMEM((cols + 1, chans, rows), f32),
                    pltpu.SMEM((most + BATCH,), jnp.int32),
                    pltpu.SMEM((cols + 1,), jnp.int32),
                    pltpu.SMEM((cols + 1,), jnp.int32),
                    pltpu.SMEM((cols + 1,), f32),
                    pltpu.SMEM((cols + 1,), f32),
                ],
                compiler_params=pltpu.CompilerParams(vmem_limit_bytes=20 * MIB),
                name="join",
            )(
                table,
                flags,
                banded.reshape(passes * ncols * slots, chans, rows),
                gains,
                t_qkv,
                t_out,
                t_in,
                w_back_t,
            )

        return run

    joined = lax.switch(
        tier[0],
        [branch(slots) for slots in range(1, per + 1)],
        packed,
        table,
        flags.T,
        gains,
        t_qkv,
        t_out,
        t_in,
        w_back_t,
    )
    return pl.pallas_call(
        functools.partial(decode_kernel, sizes[:3]),
        out_shape=shape((cols, outs, rows), f32),
        in_specs=[whole()] * 3,
        out_specs=whole(),
        scratch_shapes=[
            pltpu.VMEM((2 if dp else cols, chans, rows), half) for dp, db in MOVES
        ]
        + [
            pltpu.VMEM((cols + 4, 3 * chans, 2 * rows), half),
            pltpu.VMEM((cols + 2, 3 * chans, 2 * rows), half),
            dma((len(MOVES),)),
            dma((len(MOVES),)),
        ],
        compiler_params=pltpu.CompilerParams(
            collective_id=1, has_side_effects=True, vmem_limit_bytes=16 * MIB
        ),
        name="decode",
    )(joined, t_w1, t_w2)


def solution(mesh):
    shape = mesh.shape
    sizes = (shape["row"], shape["tile"] * shape["row"], shape["pass"], shape["groups"])
    fixed = [P()] * 12
    return jax.shard_map(
        functools.partial(local, sizes),
        mesh=mesh,
        in_specs=(
            P(("groups", "pass"), ("tile", "row"), None, None),
            P(("groups", "pass"), None),
            P("groups", ("tile", "row")),
            *fixed,
        ),
        out_specs=P(("groups", "pass"), None, ("tile", "row")),
        check_vma=False,
    )
```

```python
import functools
import math

import jax
import jax.numpy as jnp
import numpy as np
from jax import lax
from jax.experimental import pallas as pl
from jax.experimental.pallas import tpu as pltpu
from jax.sharding import PartitionSpec as P

HEADS = 4
eps = 1e-05
f32 = jnp.float32
half = jnp.bfloat16
MESH = pl.DeviceIdType.MESH
MIB = 1024 * 1024
BATCH = 8
QUERIES = 4


def whole(space=pltpu.VMEM):
    return pl.BlockSpec(memory_space=space)


def dot(weights, values):
    return jnp.dot(weights, values, preferred_element_type=f32)


def inside(col, ncols):
    return (col >= 0) & (col < ncols)


def align_kernel(sizes, shifts, x_hbm, *refs):
    hbm, refs = refs[:11], refs[11:]
    o_ref, table, tier, t_qkv, t_out, t_in, t_w1, t_w2, t_gains, foreign, picks, x_ref = refs[:12]
    vmem, (x_sem, loads, send, recv) = refs[12:23], refs[23:]
    w_query, w_key, w_value, w_out, w_in, w1, w2 = vmem[:7]
    nrow, bands, passes, groups = sizes
    _, own_cols, per, chans, rows = o_ref.shape
    ncols = own_cols * bands
    g = lax.axis_index("groups")
    p = lax.axis_index("pass")
    b = lax.axis_index("tile") * nrow + lax.axis_index("row")
    peers = [(dg, dp) for dg in range(groups) for dp in range(passes) if (dg, dp) != (0, 0)]

    def peer_id(dg, dp):
        return {"groups": (g + dg) % groups, "pass": (p + dp) % passes}

    barrier = pltpu.get_barrier_semaphore()
    for peer in peers:
        pl.semaphore_signal(barrier, inc=1, device_id=peer_id(*peer), device_id_type=MESH)
    x_copy = pltpu.make_async_copy(x_hbm, x_ref, x_sem)
    x_copy.start()
    copies = [
        pltpu.make_async_copy(hbm[n], vmem[n], loads.at[n]) for n in range(len(hbm))
    ]
    for copy in copies:
        copy.start()

    offs = [shifts[1, r] for r in range(per)]
    lanes = lax.broadcasted_iota(jnp.int32, (1, table.shape[2]), 1)
    for r in range(per):
        col = lanes + offs[r]
        slot = jnp.zeros_like(lanes)
        for q in range(r):
            slot = slot + inside(col - offs[q], ncols).astype(jnp.int32)
        live = inside(col, ncols) & (lanes < ncols)
        table[p, r : r + 1, :] = jnp.where(live, slot * ncols + col, -1)

    for c in range(own_cols):
        rank = jnp.int32(0)
        chosen = [jnp.int32(0)] * per
        for r in range(per):
            live = inside(b * own_cols + c - offs[r], ncols).astype(jnp.int32)
            for k in range(r + 1):
                chosen[k] = chosen[k] + r * live * (rank == k).astype(jnp.int32)
            rank = rank + live
        for k in range(per):
            picks[c * per + k] = chosen[k]

    if peers:
        pl.semaphore_wait(barrier, len(peers))
    pending = []
    for n, (dg, dp) in enumerate(peers):
        target = table.at[p] if dg == 0 else foreign.at[(groups - dg) % groups - 1, p]
        copy = pltpu.make_async_remote_copy(
            src_ref=table.at[p],
            dst_ref=target,
            send_sem=send.at[n],
            recv_sem=recv.at[n],
            device_id=peer_id(dg, dp),
            device_id_type=MESH,
        )
        copy.start()
        pending.append(copy)

    for copy in copies:
        copy.wait()
    for i, ref in enumerate((w_query, w_key, w_value)):
        t_qkv[i * chans : (i + 1) * chans, :] = ref[...].T
    t_out[...] = w_out[...].T
    t_in[...] = w_in[...].T
    t_w1[...] = w1[...].T
    for i, ref in enumerate(vmem[7:]):
        t_gains[i] = jnp.broadcast_to(ref[...], (rows, chans)).T
    t_w2[...] = w2[...]
    x_copy.wait()

    lane = lax.broadcasted_iota(jnp.int32, (chans, rows), 1)
    for c in range(own_cols):

        def one(k, carry):
            r = picks[c * per + k]
            offset = shifts[0, r]
            amount = lax.rem(2 * rows - offset, rows)
            pos = lane + offset
            rolled = [
                pltpu.roll(x_ref[r, c, :, t * rows : (t + 1) * rows].astype(f32), amount, 1)
                for t in range(bands)
            ]
            zero = jnp.zeros((chans, rows), f32)
            for t in range(bands):
                low = rolled[t - 1] if t else zero
                high = rolled[t + 1] if t + 1 < bands else zero
                out = jnp.where(pos < 0, low, jnp.where(pos >= rows, high, rolled[t]))
                o_ref[t, c, k] = out.astype(half)
            return carry

        lax.fori_loop(0, per, one, 0)

    for copy in pending:
        copy.wait()
    most = jnp.max(table[...])
    if groups > 1:
        most = jnp.maximum(most, jnp.max(foreign[...]))
    tier[0] = jnp.maximum(lax.div(most, ncols), 0)


def partners(b, k, bands):
    if bands & (bands - 1):
        return lax.rem(b + k, bands), lax.rem(b + bands - k, bands)
    out, bit = 0, 1
    while bit < bands:
        own = lax.rem(lax.div(b, bit), 2)
        out = out + bit * (1 - own if k // bit % 2 else own)
        bit *= 2
    return out, out


def gather_kernel(sizes, slots, s_ref, o_ref, loc, send1, recv1, send2, recv2):
    nrow, bands, passes, _ = sizes
    p = lax.axis_index("pass")
    b = lax.axis_index("tile") * nrow + lax.axis_index("row")

    def band_id(k):
        return {"tile": k // nrow, "row": k % nrow}

    barrier = pltpu.get_barrier_semaphore()
    for k in range(1, bands):
        pl.semaphore_signal(
            barrier, inc=1, device_id=band_id((b + k) % bands), device_id_type=MESH
        )
    for k in range(1, passes):
        pl.semaphore_signal(
            barrier, inc=1, device_id={"pass": (p + k) % passes}, device_id_type=MESH
        )
    own = pltpu.make_async_copy(s_ref.at[b, :, pl.ds(0, slots)], o_ref.at[p, b], loc)
    own.start()
    pl.semaphore_wait(barrier, bands + passes - 2)
    pending = []

    def forward(src, slot, index):
        for k in range(1, passes):
            copy = pltpu.make_async_remote_copy(
                src_ref=src,
                dst_ref=o_ref.at[p, index],
                send_sem=send2.at[k - 1, slot],
                recv_sem=recv2.at[k - 1, slot],
                device_id={"pass": (p + k) % passes},
                device_id_type=MESH,
            )
            copy.start()
            pending.append(copy)

    forward(s_ref.at[b, :, pl.ds(0, slots)], 0, b)
    first = []
    for k in range(1, bands):
        peer, _ = partners(b, k, bands)
        copy = pltpu.make_async_remote_copy(
            src_ref=s_ref.at[peer, :, pl.ds(0, slots)],
            dst_ref=o_ref.at[p, b],
            send_sem=send1.at[k - 1],
            recv_sem=recv1.at[k - 1],
            device_id=band_id(peer),
            device_id_type=MESH,
        )
        copy.start()
        first.append((k, copy))
    for k, copy in first:
        copy.wait_recv()
        _, source = partners(b, k, bands)
        forward(o_ref.at[p, source], k, source)
    for _, copy in first:
        copy.wait_send()
    for copy in pending:
        copy.wait()
    own.wait()


def rms(values, gain):
    mean = jnp.mean(values * values, axis=0, keepdims=True)
    return values * lax.rsqrt(mean + eps) * gain


def join_kernel(
    cols,
    ncols,
    slots,
    table,
    flags,
    x_ref,
    gains,
    w_qkv,
    w_out,
    w_in,
    w_back,
    o_ref,
    q_s,
    k_s,
    v_s,
    mixed_s,
    total_s,
    tokens,
    starts,
    lives,
    dead,
    counts,
):
    passes, per, _ = table.shape
    _, chans, rows = x_ref.shape
    count = passes * per
    head = chans // HEADS
    scale = 1.0 / math.sqrt(head)
    stride = pl.next_power_of_2(cols + 1)
    base = lax.axis_index("pass") * cols
    at = jnp.int32(0)
    for x in range(cols):
        first = at
        zeros = jnp.int32(0)
        for r in range(count):
            code = table[r // per, r % per, base + x]
            flag = flags[0, r]
            place = (r // per * ncols + lax.rem(code, ncols)) * slots + lax.div(code, ncols)
            tokens[at] = (place + 1) * stride + x
            live = flag * (code >= 0).astype(jnp.int32)
            at = at + live
            zeros = zeros + flag - live
        tokens[at] = x
        starts[x] = first
        lives[x] = at - first
        dead[x] = zeros.astype(f32)
        counts[x] = zeros.astype(f32)
        flag_sum = (at - first + zeros).astype(f32)
        at = at + 1
    for i in range(BATCH):
        tokens[at + i] = cols
    starts[cols] = 0
    lives[cols] = 0
    dead[cols] = jnp.float32(0)
    counts[cols] = jnp.float32(1)
    batches = lax.div(at + BATCH - 1, BATCH)

    def cell_of(t):
        place = lax.div(tokens[t], stride) - 1
        return jnp.where(place >= 0, x_ref[jnp.maximum(place, 0)].astype(f32), 0.0)

    def part(values, i):
        return values[:, i * rows : (i + 1) * rows]

    def project(j, carry):
        g1, gq, gk = gains[0], gains[1], gains[2]
        normed = [rms(cell_of(j * BATCH + i), g1).astype(half) for i in range(BATCH)]
        qkv = dot(w_qkv[...], jnp.concatenate(normed, axis=1))
        for i in range(BATCH):
            one = part(qkv, i)
            t = j * BATCH + i
            q_s[t] = rms(one[:chans], gq).astype(half).astype(f32) * scale
            k_s[t] = rms(one[chans : 2 * chans], gk).astype(half).astype(f32)
            v_s[t] = one[2 * chans :].astype(half).astype(f32)
        return carry

    lax.fori_loop(0, batches, project, 0)
    total_s[...] = jnp.zeros_like(total_s)

    def attend(j, carry):
        for i0 in range(0, BATCH, QUERIES):
            owner = [lax.rem(tokens[j * BATCH + i0 + i], stride) for i in range(QUERIES)]
            begin = [starts[x] for x in owner]
            size = [lives[x] for x in owner]
            longest = functools.reduce(jnp.maximum, size)

            def keys_of(k, sums):
                out = []
                for i in range(QUERIES):
                    above, below = sums[i]
                    at = begin[i] + jnp.maximum(jnp.minimum(k, size[i] - 1), 0)
                    prod = (q_s[j * BATCH + i0 + i] * k_s[at]).reshape(HEADS, head, rows)
                    weight = jnp.exp(jnp.sum(prod, axis=1, keepdims=True))
                    weight = weight * jnp.where(k < size[i], 1.0, 0.0)
                    value = v_s[at].reshape(HEADS, head, rows)
                    out.append((above + weight * value, below + weight))
                return tuple(out)

            init = tuple(
                (
                    jnp.zeros((HEADS, head, rows), f32),
                    jnp.full((HEADS, 1, rows), counts[owner[i]], f32),
                )
                for i in range(QUERIES)
            )
            sums = lax.fori_loop(0, longest, keys_of, init)
            for i in range(QUERIES):
                above, below = sums[i]
                mixed = (above * (1.0 / below)).reshape(chans, rows).astype(half)
                mixed_s[:, (i0 + i) * rows : (i0 + i + 1) * rows] = mixed
        back = dot(w_out[...], mixed_s[...])
        g2 = gains[3]
        hidden = [cell_of(j * BATCH + i) + part(back, i) for i in range(BATCH)]
        normed = [rms(one, g2).astype(half) for one in hidden]
        inner = jax.nn.gelu(dot(w_in[...], jnp.concatenate(normed, axis=1)), approximate=True)
        added = dot(w_back[...], inner.astype(half))
        for i in range(BATCH):
            token = tokens[j * BATCH + i]
            x = lax.rem(token, stride)
            weight = jnp.where(token >= stride, 1.0, dead[x])
            total_s[x] += (hidden[i] + part(added, i)) * weight
        return carry

    lax.fori_loop(0, batches, attend, 0)
    for x in range(cols):
        o_ref[x] = (total_s[x] / flag_sum).astype(half)


MOVES = [(dp, db) for dp in (-1, 0, 1) for db in (-1, 0, 1) if (dp, db) != (0, 0)]


def decode_kernel(sizes, j_ref, w1, w2, o_ref, *scratch):
    nrow, bands, passes = sizes
    bufs = scratch[: len(MOVES)]
    taps, acts, send, recv = scratch[len(MOVES) :]
    cols, chans, rows = j_ref.shape
    p = lax.axis_index("pass")
    b = lax.axis_index("tile") * nrow + lax.axis_index("row")

    def exists(dp, db):
        ok = jnp.bool_(True)
        if dp:
            ok = ok & (p + dp >= 0) & (p + dp < passes)
        if db:
            ok = ok & (b + db >= 0) & (b + db < bands)
        return ok

    def target(dp, db):
        k = b + db
        return {"pass": p + dp, "tile": k // nrow, "row": k % nrow}

    barrier = pltpu.get_barrier_semaphore()
    neighbours = jnp.int32(0)
    for dp, db in MOVES:
        there = exists(dp, db)
        neighbours = neighbours + there.astype(jnp.int32)

        @pl.when(there)
        def _():
            pl.semaphore_signal(barrier, inc=1, device_id=target(dp, db), device_id_type=MESH)

    pl.semaphore_wait(barrier, neighbours)

    def copy_of(n):
        dp, db = MOVES[n]
        src = j_ref
        if dp:
            src = j_ref.at[pl.ds(cols - 2 if dp > 0 else 0, 2)]
        return pltpu.make_async_remote_copy(
            src_ref=src,
            dst_ref=bufs[n],
            send_sem=send.at[n],
            recv_sem=recv.at[n],
            device_id=target(dp, db),
            device_id_type=MESH,
        )

    for n, (dp, db) in enumerate(MOVES):

        @pl.when(exists(dp, db))
        def _():
            copy_of(n).start()

    for n, (dp, db) in enumerate(MOVES):

        @pl.when(exists(-dp, -db))
        def _():
            copy_of(n).wait_recv()

        @pl.when(jnp.logical_not(exists(-dp, -db)))
        def _():
            bufs[n][...] = jnp.zeros_like(bufs[n])

    def side(dp, db):
        return bufs[MOVES.index((-dp, -db))]

    lane = lax.broadcasted_iota(jnp.int32, (chans, rows), 1)
    wide_lane = lax.broadcasted_iota(jnp.int32, (chans, 2 * rows), 1)

    def widen(values):
        last = 2 * rows - 1
        return jnp.concatenate(
            [
                pltpu.roll(values, 1, 1).astype(half),
                values.astype(half),
                pltpu.roll(values, last, 1).astype(half),
            ],
            axis=0,
        )

    for n in range(cols + 4):
        dp = -1 if n < 2 else (1 if n >= cols + 2 else 0)
        at = n if dp < 0 else (n - cols - 2 if dp > 0 else n - 2)
        middle = j_ref[at] if dp == 0 else side(dp, 0)[at]
        border = jnp.where(
            lane < rows // 2, side(dp, 1)[at].astype(f32), side(dp, -1)[at].astype(f32)
        )
        taps[n] = widen(jnp.concatenate([middle.astype(f32), border], axis=1))
    row_pos = b * rows + jnp.where(wide_lane < rows + rows // 2, wide_lane, wide_lane - 2 * rows)
    row_inside = (row_pos >= 0) & (row_pos < bands * rows)
    for n in range(cols + 2):
        near = taps[n : n + 3].reshape(9 * chans, 2 * rows)
        act = jax.nn.gelu(dot(w1[...], near), approximate=True)
        col_pos = p * cols + n - 1
        inside = row_inside & (col_pos >= 0) & (col_pos < passes * cols)
        acts[n] = widen(jnp.where(inside, act, 0.0))
    for n in range(cols):
        near = acts[n : n + 3, :, :rows].reshape(9 * chans, rows)
        o_ref[n] = dot(w2[...], near)

    for n, (dp, db) in enumerate(MOVES):

        @pl.when(exists(dp, db))
        def _():
            copy_of(n).wait_send()


def local(
    sizes,
    revisits,
    shifts,
    flags,
    norm1_gain,
    w_query,
    w_key,
    w_value,
    query_gain,
    key_gain,
    w_out,
    norm2_gain,
    w_in,
    w_back,
    conv_first,
    conv_second,
):
    nrow, bands, passes, groups = sizes
    per, own_cols, chans, all_rows = revisits.shape
    rows = all_rows // bands
    ncols = own_cols * bands
    cols = ncols // passes
    count = per * passes
    outs = conv_second.shape[3]
    hidden = w_in.shape[1]
    dma = pltpu.SemaphoreType.DMA
    peers = max(groups * passes - 1, 1)
    shape = jax.ShapeDtypeStruct
    prepared = (
        w_query,
        w_key,
        w_value,
        w_out,
        w_in,
        conv_first.reshape(9 * chans, -1),
        conv_second.transpose(3, 0, 1, 2).reshape(outs, 9 * chans),
        *(gain.reshape(1, chans) for gain in (norm1_gain, query_gain, key_gain, norm2_gain)),
    )
    outputs = (
        shape((bands, own_cols, per, chans, rows), half),
        shape((passes, per, 128), jnp.int32),
        shape((1,), jnp.int32),
        shape((3 * chans, chans), half),
        shape((chans, chans), half),
        shape((hidden, chans), half),
        shape((chans, 9 * chans), half),
        shape((outs, 9 * chans), half),
        shape((4, chans, rows), f32),
    )
    packed, table, tier, t_qkv, t_out, t_in, t_w1, t_w2, gains = pl.pallas_call(
        functools.partial(align_kernel, sizes),
        out_shape=outputs,
        in_specs=[whole(pltpu.SMEM)] + [whole(pltpu.HBM)] * 12,
        out_specs=tuple(whole(pltpu.SMEM) if n == 2 else whole() for n in range(len(outputs))),
        scratch_shapes=[
            pltpu.VMEM((max(groups - 1, 1), passes, per, 128), jnp.int32),
            pltpu.SMEM((own_cols * per,), jnp.int32),
            pltpu.VMEM(revisits.shape, half),
            *(pltpu.VMEM(array.shape, array.dtype) for array in prepared),
            dma,
            dma((len(prepared),)),
            dma((peers,)),
            dma((peers,)),
        ],
        compiler_params=pltpu.CompilerParams(
            collective_id=0, has_side_effects=True, vmem_limit_bytes=16 * MIB
        ),
        name="align",
    )(shifts.T, *(pltpu.with_memory_space_constraint(a, pltpu.HBM) for a in (revisits, *prepared)))
    others = max(passes - 1, 1)
    most = cols * (count + 1)
    room = (most + BATCH - 1) // BATCH * BATCH
    w_back_t = w_back.T

    def branch(slots):
        def run(packed, table, flags, gains, t_qkv, t_out, t_in, w_back_t):
            banded = pl.pallas_call(
                functools.partial(gather_kernel, sizes, slots),
                out_shape=shape((passes, bands, own_cols, slots, chans, rows), half),
                in_specs=[whole(pl.ANY)],
                out_specs=whole(),
                scratch_shapes=[
                    dma,
                    dma((bands,)),
                    dma((bands,)),
                    dma((others, bands)),
                    dma((others, bands)),
                ],
                compiler_params=pltpu.CompilerParams(
                    collective_id=2 + slots, has_side_effects=True, vmem_limit_bytes=16 * MIB
                ),
                name="exchange",
            )(packed)
            return pl.pallas_call(
                functools.partial(join_kernel, cols, ncols, slots),
                out_shape=shape((cols, chans, rows), half),
                in_specs=[whole(pltpu.SMEM), whole(pltpu.SMEM)] + [whole()] * 6,
                out_specs=whole(),
                scratch_shapes=[
                    pltpu.VMEM((room, chans, rows), f32),
                    pltpu.VMEM((room, chans, rows), f32),
                    pltpu.VMEM((room, chans, rows), f32),
                    pltpu.VMEM((chans, BATCH * rows), half),
                    pltpu.VMEM((cols + 1, chans, rows), f32),
                    pltpu.SMEM((most + BATCH,), jnp.int32),
                    pltpu.SMEM((cols + 1,), jnp.int32),
                    pltpu.SMEM((cols + 1,), jnp.int32),
                    pltpu.SMEM((cols + 1,), f32),
                    pltpu.SMEM((cols + 1,), f32),
                ],
                compiler_params=pltpu.CompilerParams(vmem_limit_bytes=20 * MIB),
                name="join",
            )(
                table,
                flags,
                banded.reshape(passes * ncols * slots, chans, rows),
                gains,
                t_qkv,
                t_out,
                t_in,
                w_back_t,
            )

        return run

    joined = lax.switch(
        tier[0],
        [branch(slots) for slots in range(1, per + 1)],
        packed,
        table,
        flags.T,
        gains,
        t_qkv,
        t_out,
        t_in,
        w_back_t,
    )
    return pl.pallas_call(
        functools.partial(decode_kernel, sizes[:3]),
        out_shape=shape((cols, outs, rows), f32),
        in_specs=[whole()] * 3,
        out_specs=whole(),
        scratch_shapes=[
            pltpu.VMEM((2 if dp else cols, chans, rows), half) for dp, db in MOVES
        ]
        + [
            pltpu.VMEM((cols + 4, 3 * chans, 2 * rows), half),
            pltpu.VMEM((cols + 2, 3 * chans, 2 * rows), half),
            dma((len(MOVES),)),
            dma((len(MOVES),)),
        ],
        compiler_params=pltpu.CompilerParams(
            collective_id=1, has_side_effects=True, vmem_limit_bytes=16 * MIB
        ),
        name="decode",
    )(joined, t_w1, t_w2)


def solution(mesh):
    shape = mesh.shape
    sizes = (shape["row"], shape["tile"] * shape["row"], shape["pass"], shape["groups"])
    fixed = [P()] * 12
    return jax.shard_map(
        functools.partial(local, sizes),
        mesh=mesh,
        in_specs=(
            P(("groups", "pass"), ("tile", "row"), None, None),
            P(("groups", "pass"), None),
            P("groups", ("tile", "row")),
            *fixed,
        ),
        out_specs=P(("groups", "pass"), None, ("tile", "row")),
        check_vma=False,
    )
```

```python
import functools
import math

import jax
import jax.numpy as jnp
import numpy as np
from jax import lax
from jax.experimental import pallas as pl
from jax.experimental.pallas import tpu as pltpu
from jax.sharding import PartitionSpec as P

HEADS = 4
eps = 1e-05
f32 = jnp.float32
half = jnp.bfloat16
MESH = pl.DeviceIdType.MESH
MIB = 1024 * 1024
BATCH = 8
QUERIES = 2


def whole(space=pltpu.VMEM):
    return pl.BlockSpec(memory_space=space)


def dot(weights, values):
    return jnp.dot(weights, values, preferred_element_type=f32)


GELU = math.sqrt(2.0 / math.pi)


def gelu(x):
    shaped = x * (GELU + (GELU * 0.044715) * (x * x))
    halved = 0.5 * x
    return halved + halved * jnp.tanh(shaped)


def inside(col, ncols):
    return (col >= 0) & (col < ncols)


def align_kernel(sizes, *refs):
    hbm, refs = refs[:13], refs[13:]
    x_ref, table, picks, tier, t_qkv, t_out, t_in, t_w1, t_w2, t_gains = refs[:10]
    foreign, shifts, *vmem = refs[10:23]
    loads, send, recv = refs[23:]
    w_query, w_key, w_value, w_out, w_in, w1, w2 = vmem[:7]
    nrow, bands, passes, groups = sizes
    per, own_cols, chans, _ = x_ref.shape
    rows = t_gains.shape[2]
    ncols = own_cols * bands
    g = lax.axis_index("groups")
    p = lax.axis_index("pass")
    b = lax.axis_index("tile") * nrow + lax.axis_index("row")
    peers = [(dg, dp) for dg in range(groups) for dp in range(passes) if (dg, dp) != (0, 0)]

    def peer_id(dg, dp):
        return {"groups": (g + dg) % groups, "pass": (p + dp) % passes}

    barrier = pltpu.get_barrier_semaphore()
    for peer in peers:
        pl.semaphore_signal(barrier, inc=1, device_id=peer_id(*peer), device_id_type=MESH)
    copies = [
        pltpu.make_async_copy(source, target, loads.at[n])
        for n, (source, target) in enumerate(zip(hbm, [shifts, x_ref, *vmem]))
    ]
    for copy in copies:
        copy.start()
    copies[0].wait()

    offs = [shifts[1, r] for r in range(per)]
    lanes = lax.broadcasted_iota(jnp.int32, (1, table.shape[2]), 1)
    for r in range(per):
        col = lanes + offs[r]
        slot = jnp.zeros_like(lanes)
        for q in range(r):
            slot = slot + inside(col - offs[q], ncols).astype(jnp.int32)
        live = inside(col, ncols) & (lanes < ncols)
        table[p, r : r + 1, :] = jnp.where(live, slot * ncols + col, -1)

    for c in range(own_cols):
        rank = jnp.int32(0)
        chosen = [jnp.int32(0)] * per
        for r in range(per):
            live = inside(b * own_cols + c - offs[r], ncols).astype(jnp.int32)
            for k in range(r + 1):
                chosen[k] = chosen[k] + r * live * (rank == k).astype(jnp.int32)
            rank = rank + live
        for k in range(per):
            picks[0, c * per + k] = chosen[k]
            picks[1, c * per + k] = shifts[0, chosen[k]]

    if peers:
        pl.semaphore_wait(barrier, len(peers))
    pending = []
    for n, (dg, dp) in enumerate(peers):
        target = table.at[p] if dg == 0 else foreign.at[(groups - dg) % groups - 1, p]
        copy = pltpu.make_async_remote_copy(
            src_ref=table.at[p],
            dst_ref=target,
            send_sem=send.at[n],
            recv_sem=recv.at[n],
            device_id=peer_id(dg, dp),
            device_id_type=MESH,
        )
        copy.start()
        pending.append(copy)

    for copy in copies[2:]:
        copy.wait()
    for i, ref in enumerate((w_query, w_key, w_value)):
        t_qkv[i * chans : (i + 1) * chans, :] = ref[...].T
    t_out[...] = w_out[...].T
    t_in[...] = w_in[...].T
    t_w1[...] = w1[...].T
    for i, ref in enumerate(vmem[7:]):
        t_gains[i] = jnp.broadcast_to(ref[...], (rows, chans)).T
    for i in range(w2.shape[0]):
        taps = w2[i].astype(f32)
        for j in range(w2.shape[2]):
            at = (i * w2.shape[2] + j) * chans
            t_w2[:, at : at + chans] = taps[:, j, :].astype(half)
    copies[1].wait()
    for copy in pending:
        copy.wait()
    most = jnp.max(table[...])
    if groups > 1:
        most = jnp.maximum(most, jnp.max(foreign[...]))
    tier[0] = jnp.maximum(lax.div(most, ncols), 0)


def partners(b, k, bands):
    if bands & (bands - 1):
        return lax.rem(b + k, bands), lax.rem(b + bands - k, bands)
    out, bit = 0, 1
    while bit < bands:
        own = lax.rem(lax.div(b, bit), 2)
        out = out + bit * (1 - own if k // bit % 2 else own)
        bit *= 2
    return out, out


def gather_kernel(sizes, slots, *refs):
    meta, (x_ref, o_ref, list_ref, packed), refs = refs[:3], refs[3:7], refs[7:]
    (picks, table, flags), (small, loc, send1, recv1, send2, recv2) = refs[:3], refs[3:]
    nrow, bands, passes, _ = sizes
    per, own_cols, _, _ = x_ref.shape
    chans, rows = o_ref.shape[4:]
    ncols = own_cols * bands
    cols = ncols // passes
    p = lax.axis_index("pass")
    b = lax.axis_index("tile") * nrow + lax.axis_index("row")

    def band_id(k):
        return {"tile": k // nrow, "row": k % nrow}

    barrier = pltpu.get_barrier_semaphore()
    for k in range(1, bands):
        pl.semaphore_signal(
            barrier, inc=1, device_id=band_id((b + k) % bands), device_id_type=MESH
        )
    for k in range(1, passes):
        pl.semaphore_signal(
            barrier, inc=1, device_id={"pass": (p + k) % passes}, device_id_type=MESH
        )
    copies = [
        pltpu.make_async_copy(source, target, small.at[n])
        for n, (source, target) in enumerate(zip(meta, (picks, table, flags)))
    ]
    for copy in copies:
        copy.start()
    for copy in copies:
        copy.wait()

    lane = lax.broadcasted_iota(jnp.int32, (chans, rows), 1)
    zero = jnp.zeros((chans, rows), f32)
    for c in range(own_cols):
        for k in range(slots):
            r = picks[0, c * per + k]
            offset = picks[1, c * per + k]
            amount = lax.rem(2 * rows - offset, rows)
            pos = lane + offset
            rolled = [
                pltpu.roll(x_ref[r, c, :, t * rows : (t + 1) * rows].astype(f32), amount, 1)
                for t in range(bands)
            ]
            for t in range(bands):
                low = rolled[t - 1] if t else zero
                high = rolled[t + 1] if t + 1 < bands else zero
                out = jnp.where(pos < 0, low, jnp.where(pos >= rows, high, rolled[t]))
                packed[t, c, k] = out.astype(half)

    count = passes * per
    stride = pl.next_power_of_2(cols + 1)
    spots = lax.broadcasted_iota(jnp.int32, (1, list_ref.shape[1]), 1)
    token = jnp.full_like(spots, cols)
    start = jnp.zeros_like(spots)
    size = jnp.zeros_like(spots)
    below = jnp.full_like(spots, 1)
    weight = jnp.zeros_like(spots)
    at = jnp.int32(0)
    for x in range(cols):
        first = at
        total = jnp.int32(0)
        for r in range(count):
            code = table[r // per, r % per, p * cols + x]
            flag = flags[0, r]
            place = (r // per * ncols + lax.rem(code, ncols)) * slots + lax.div(code, ncols)
            token = jnp.where(spots == at, (place + 1) * stride + x, token)
            at = at + flag * (code >= 0).astype(jnp.int32)
            total = total + flag
        dead = total - (at - first)
        token = jnp.where(spots == at, x, token)
        here = (spots >= first) & (spots <= at)
        start = jnp.where(here, first, start)
        size = jnp.where(here, at - first, size)
        below = jnp.where(here, dead, below)
        weight = jnp.where(here, jnp.where(spots == at, dead, 1), weight)
        at = at + 1
    for n, value in enumerate((token, start, size, below, weight)):
        list_ref[n : n + 1, :] = value
    list_ref[5:6, :] = jnp.full_like(spots, at)
    list_ref[6:7, :] = jnp.full_like(spots, total)

    pl.semaphore_wait(barrier, bands + passes - 2)
    own = pltpu.make_async_copy(packed.at[b], o_ref.at[p, b], loc)
    own.start()
    pending = []

    def forward(src, slot, index):
        for k in range(1, passes):
            copy = pltpu.make_async_remote_copy(
                src_ref=src,
                dst_ref=o_ref.at[p, index],
                send_sem=send2.at[k - 1, slot],
                recv_sem=recv2.at[k - 1, slot],
                device_id={"pass": (p + k) % passes},
                device_id_type=MESH,
            )
            copy.start()
            pending.append(copy)

    forward(packed.at[b], 0, b)
    first = []
    for k in range(1, bands):
        peer, _ = partners(b, k, bands)
        copy = pltpu.make_async_remote_copy(
            src_ref=packed.at[peer],
            dst_ref=o_ref.at[p, b],
            send_sem=send1.at[k - 1],
            recv_sem=recv1.at[k - 1],
            device_id=band_id(peer),
            device_id_type=MESH,
        )
        copy.start()
        first.append((k, copy))
    for k, copy in first:
        copy.wait_recv()
        _, source = partners(b, k, bands)
        forward(o_ref.at[p, source], k, source)
    for _, copy in first:
        copy.wait_send()
    for copy in pending:
        copy.wait()
    own.wait()


def rms(values, gain):
    mean = jnp.mean(values * values, axis=0, keepdims=True)
    return values * lax.rsqrt(mean + eps) * gain


def join_kernel(
    cols,
    tokens,
    x_ref,
    gains,
    w_qkv,
    w_out,
    w_in,
    w_back,
    o_ref,
    edges,
    q_s,
    k_s,
    v_s,
    mixed_s,
    total_s,
):
    _, chans, rows = x_ref.shape
    head = chans // HEADS
    scale = 1.0 / math.sqrt(head)
    stride = pl.next_power_of_2(cols + 1)
    batches = lax.div(tokens[5, 0] + BATCH - 1, BATCH)

    def cell_of(t):
        place = lax.div(tokens[0, t], stride) - 1
        return jnp.where(place >= 0, x_ref[jnp.maximum(place, 0)].astype(f32), 0.0)

    def part(values, i):
        return values[:, i * rows : (i + 1) * rows]

    def project(j, carry):
        g1, gq, gk = gains[0], gains[1], gains[2]
        normed = [rms(cell_of(j * BATCH + i), g1).astype(half) for i in range(BATCH)]
        qkv = dot(w_qkv[...], jnp.concatenate(normed, axis=1))
        for i in range(BATCH):
            one = part(qkv, i)
            t = j * BATCH + i
            q_s[t] = rms(one[:chans], gq * scale)
            k_s[t] = rms(one[chans : 2 * chans], gk)
            v_s[t] = one[2 * chans :]
        return carry

    lax.fori_loop(0, batches, project, 0)
    total_s[...] = jnp.zeros_like(total_s)

    def attend(j, carry):
        for i0 in range(0, BATCH, QUERIES):
            mine = [j * BATCH + i0 + i for i in range(QUERIES)]
            begin = [tokens[1, t] for t in mine]
            size = [tokens[2, t] for t in mine]
            longest = functools.reduce(jnp.maximum, size)

            def keys_of(k, sums):
                out = []
                for i in range(QUERIES):
                    above, below = sums[i]
                    at = begin[i] + jnp.maximum(jnp.minimum(k, size[i] - 1), 0)
                    prod = (q_s[mine[i]] * k_s[at]).reshape(HEADS, head, rows)
                    weight = jnp.exp(jnp.sum(prod, axis=1, keepdims=True))
                    weight = weight * jnp.where(k < size[i], 1.0, 0.0)
                    value = v_s[at].reshape(HEADS, head, rows)
                    out.append((above + weight * value, below + weight))
                return tuple(out)

            init = tuple(
                (
                    jnp.zeros((HEADS, head, rows), f32),
                    jnp.full((HEADS, 1, rows), tokens[3, t].astype(f32), f32),
                )
                for t in mine
            )
            sums = lax.fori_loop(0, longest, keys_of, init)
            for i in range(QUERIES):
                above, below = sums[i]
                mixed = (above * (1.0 / below)).reshape(chans, rows).astype(half)
                mixed_s[:, (i0 + i) * rows : (i0 + i + 1) * rows] = mixed
        back = dot(w_out[...], mixed_s[...])
        g2 = gains[3]
        hidden = [cell_of(j * BATCH + i) + part(back, i) for i in range(BATCH)]
        normed = [rms(one, g2).astype(half) for one in hidden]
        inner = gelu(dot(w_in[...], jnp.concatenate(normed, axis=1)))
        added = dot(w_back[...], inner.astype(half))
        for i in range(BATCH):
            t = j * BATCH + i
            x = lax.rem(tokens[0, t], stride)
            total_s[x] += (hidden[i] + part(added, i)) * tokens[4, t].astype(f32)
        return carry

    lax.fori_loop(0, batches, attend, 0)
    flag_sum = tokens[6, 0].astype(f32)
    width = rows // cols
    lane = lax.broadcasted_iota(jnp.int32, (chans, rows), 1)
    top = bottom = jnp.zeros((chans, rows), f32)
    for x in range(cols):
        joined = total_s[x] / flag_sum
        o_ref[x] = joined.astype(half)
        here = (lane >= x * width) & (lane < (x + 1) * width)
        top = jnp.where(here, pltpu.roll(joined, x * width, 1), top)
        bottom = jnp.where(here, pltpu.roll(joined, (x + 1) * width % rows, 1), bottom)
    edges[0] = top.astype(half)
    edges[1] = bottom.astype(half)


MOVES = [(dp, db) for dp in (-1, 0, 1) for db in (-1, 0, 1) if (dp, db) != (0, 0)]


def decode_kernel(sizes, j_ref, edges, w1, w2, o_ref, *scratch):
    nrow, bands, passes = sizes
    bufs = scratch[: len(MOVES)]
    taps, acts, send, recv = scratch[len(MOVES) :]
    cols, chans, rows = j_ref.shape
    p = lax.axis_index("pass")
    b = lax.axis_index("tile") * nrow + lax.axis_index("row")

    def exists(dp, db):
        ok = jnp.bool_(True)
        if dp:
            ok = ok & (p + dp >= 0) & (p + dp < passes)
        if db:
            ok = ok & (b + db >= 0) & (b + db < bands)
        return ok

    def target(dp, db):
        k = b + db
        return {"pass": p + dp, "tile": k // nrow, "row": k % nrow}

    barrier = pltpu.get_barrier_semaphore()
    neighbours = jnp.int32(0)
    for dp, db in MOVES:
        there = exists(dp, db)
        neighbours = neighbours + there.astype(jnp.int32)

        @pl.when(there)
        def _():
            pl.semaphore_signal(barrier, inc=1, device_id=target(dp, db), device_id_type=MESH)

    pl.semaphore_wait(barrier, neighbours)

    def copy_of(n):
        dp, db = MOVES[n]
        if db:
            src = edges.at[0 if db < 0 else 1]
        else:
            src = j_ref.at[pl.ds(cols - 2 if dp > 0 else 0, 2)]
        return pltpu.make_async_remote_copy(
            src_ref=src,
            dst_ref=bufs[n],
            send_sem=send.at[n],
            recv_sem=recv.at[n],
            device_id=target(dp, db),
            device_id_type=MESH,
        )

    for n, (dp, db) in enumerate(MOVES):

        @pl.when(exists(dp, db))
        def _():
            copy_of(n).start()

    for n, (dp, db) in enumerate(MOVES):

        @pl.when(exists(-dp, -db))
        def _():
            copy_of(n).wait_recv()

        @pl.when(jnp.logical_not(exists(-dp, -db)))
        def _():
            bufs[n][...] = jnp.zeros_like(bufs[n])

    def side(dp, db):
        return bufs[MOVES.index((-dp, -db))]

    lane = lax.broadcasted_iota(jnp.int32, (chans, rows), 1)
    wide_lane = lax.broadcasted_iota(jnp.int32, (chans, 2 * rows), 1)

    def widen(values):
        last = 2 * rows - 1
        return jnp.concatenate(
            [
                pltpu.roll(values, 1, 1).astype(half),
                values.astype(half),
                pltpu.roll(values, last, 1).astype(half),
            ],
            axis=0,
        )

    width = rows // cols
    for n in range(cols + 4):
        dp = -1 if n < 2 else (1 if n >= cols + 2 else 0)
        at = n if dp < 0 else (n - cols - 2 if dp > 0 else n - 2)
        middle = j_ref[at] if dp == 0 else side(dp, 0)[at]
        col = cols - 2 + n if dp < 0 else at
        after = pltpu.roll(side(dp, 1)[...].astype(f32), (rows - col * width) % rows, 1)
        before = pltpu.roll(side(dp, -1)[...].astype(f32), rows - (col + 1) * width, 1)
        border = jnp.where(lane < rows // 2, after, before)
        taps[n] = widen(jnp.concatenate([middle.astype(f32), border], axis=1))
    row_pos = b * rows + jnp.where(wide_lane < rows + rows // 2, wide_lane, wide_lane - 2 * rows)
    row_inside = (row_pos >= 0) & (row_pos < bands * rows)
    for n in range(cols + 2):
        near = taps[n : n + 3].reshape(9 * chans, 2 * rows)
        act = gelu(dot(w1[...], near))
        col_pos = p * cols + n - 1
        inside = row_inside & (col_pos >= 0) & (col_pos < passes * cols)
        acts[n] = widen(jnp.where(inside, act, 0.0))
    for n in range(cols):
        near = acts[n : n + 3, :, :rows].reshape(9 * chans, rows)
        o_ref[n] = dot(w2[...], near)

    for n, (dp, db) in enumerate(MOVES):

        @pl.when(exists(dp, db))
        def _():
            copy_of(n).wait_send()


def local(
    sizes,
    revisits,
    shifts,
    flags,
    norm1_gain,
    w_query,
    w_key,
    w_value,
    query_gain,
    key_gain,
    w_out,
    norm2_gain,
    w_in,
    w_back,
    conv_first,
    conv_second,
):
    nrow, bands, passes, groups = sizes
    per, own_cols, chans, all_rows = revisits.shape
    rows = all_rows // bands
    ncols = own_cols * bands
    cols = ncols // passes
    count = per * passes
    outs = conv_second.shape[3]
    hidden = w_in.shape[1]
    dma = pltpu.SemaphoreType.DMA
    peers = max(groups * passes - 1, 1)
    shape = jax.ShapeDtypeStruct
    operands = (
        shifts.T,
        revisits,
        w_query,
        w_key,
        w_value,
        w_out,
        w_in,
        conv_first.reshape(9 * chans, -1),
        conv_second.transpose(0, 3, 1, 2),
        *(gain.reshape(1, chans) for gain in (norm1_gain, query_gain, key_gain, norm2_gain)),
    )
    results = (
        shape(revisits.shape, half),
        shape((passes, per, 128), jnp.int32),
        shape((2, own_cols * per), jnp.int32),
        shape((1,), jnp.int32),
        shape((3 * chans, chans), half),
        shape((chans, chans), half),
        shape((hidden, chans), half),
        shape((chans, 9 * chans), half),
        shape((outs, 9 * chans), half),
        shape((4, chans, rows), f32),
    )
    x, table, picks, tier, t_qkv, t_out, t_in, t_w1, t_w2, gains = pl.pallas_call(
        functools.partial(align_kernel, sizes),
        out_shape=results,
        in_specs=[whole(pltpu.HBM)] * len(operands),
        out_specs=tuple(whole(pltpu.SMEM) if n in (2, 3) else whole() for n in range(len(results))),
        scratch_shapes=[
            pltpu.VMEM((max(groups - 1, 1), passes, per, 128), jnp.int32),
            pltpu.SMEM((2, per), jnp.int32),
            *(pltpu.VMEM(array.shape, array.dtype) for array in operands[2:]),
            dma((len(operands),)),
            dma((peers,)),
            dma((peers,)),
        ],
        compiler_params=pltpu.CompilerParams(
            collective_id=0, has_side_effects=True, vmem_limit_bytes=16 * MIB
        ),
        name="align",
    )(*(pltpu.with_memory_space_constraint(array, pltpu.HBM) for array in operands))
    others = max(passes - 1, 1)
    most = cols * (count + 1)
    room = (most + BATCH - 1) // BATCH * BATCH
    width = (most + BATCH + 127) // 128 * 128

    def branch(slots):
        def run(picks, table, flags, x, gains, t_qkv, t_out, t_in, w_back_t):
            banded, tokens = pl.pallas_call(
                functools.partial(gather_kernel, sizes, slots),
                out_shape=(
                    shape((passes, bands, own_cols, slots, chans, rows), half),
                    shape((8, width), jnp.int32),
                ),
                in_specs=[whole(pl.ANY)] * 3 + [whole()],
                out_specs=(whole(), whole()),
                scratch_shapes=[
                    pltpu.VMEM((bands, own_cols, slots, chans, rows), half),
                    pltpu.SMEM(picks.shape, jnp.int32),
                    pltpu.SMEM(table.shape, jnp.int32),
                    pltpu.SMEM(flags.shape, jnp.int32),
                    dma((3,)),
                    dma,
                    dma((bands,)),
                    dma((bands,)),
                    dma((others, bands)),
                    dma((others, bands)),
                ],
                compiler_params=pltpu.CompilerParams(
                    collective_id=2 + slots, has_side_effects=True, vmem_limit_bytes=16 * MIB
                ),
                name="exchange",
            )(picks, table, flags, x)
            return pl.pallas_call(
                functools.partial(join_kernel, cols),
                out_shape=(
                    shape((cols, chans, rows), half),
                    shape((2, chans, rows), half),
                ),
                in_specs=[whole(pltpu.SMEM)] + [whole()] * 6,
                out_specs=(whole(), whole()),
                scratch_shapes=[
                    pltpu.VMEM((room, chans, rows), f32),
                    pltpu.VMEM((room, chans, rows), f32),
                    pltpu.VMEM((room, chans, rows), f32),
                    pltpu.VMEM((chans, BATCH * rows), half),
                    pltpu.VMEM((cols + 1, chans, rows), f32),
                ],
                compiler_params=pltpu.CompilerParams(vmem_limit_bytes=20 * MIB),
                name="join",
            )(
                tokens,
                banded.reshape(passes * ncols * slots, chans, rows),
                gains,
                t_qkv,
                t_out,
                t_in,
                w_back_t,
            )

        return run

    joined, edges = lax.switch(
        tier[0],
        [branch(slots) for slots in range(1, per + 1)],
        picks,
        table,
        flags.T,
        x,
        gains,
        t_qkv,
        t_out,
        t_in,
        w_back.T,
    )
    return pl.pallas_call(
        functools.partial(decode_kernel, sizes[:3]),
        out_shape=shape((cols, outs, rows), f32),
        in_specs=[whole()] * 4,
        out_specs=whole(),
        scratch_shapes=[
            pltpu.VMEM((chans, rows) if db else (2, chans, rows), half) for dp, db in MOVES
        ]
        + [
            pltpu.VMEM((cols + 4, 3 * chans, 2 * rows), half),
            pltpu.VMEM((cols + 2, 3 * chans, 2 * rows), half),
            dma((len(MOVES),)),
            dma((len(MOVES),)),
        ],
        compiler_params=pltpu.CompilerParams(
            collective_id=1, has_side_effects=True, vmem_limit_bytes=16 * MIB
        ),
        name="decode",
    )(joined, edges, t_w1, t_w2)


def solution(mesh):
    shape = mesh.shape
    sizes = (shape["row"], shape["tile"] * shape["row"], shape["pass"], shape["groups"])
    fixed = [P()] * 12
    return jax.shard_map(
        functools.partial(local, sizes),
        mesh=mesh,
        in_specs=(
            P(("groups", "pass"), ("tile", "row"), None, None),
            P(("groups", "pass"), None),
            P("groups", ("tile", "row")),
            *fixed,
        ),
        out_specs=P(("groups", "pass"), None, ("tile", "row")),
        check_vma=False,
    )
```

```python
import functools
import math

import jax
import jax.numpy as jnp
import numpy as np
from jax import lax
from jax.experimental import pallas as pl
from jax.experimental.pallas import tpu as pltpu
from jax.sharding import PartitionSpec as P

HEADS = 4
eps = 1e-05
f32 = jnp.float32
half = jnp.bfloat16
MESH = pl.DeviceIdType.MESH
MIB = 1024 * 1024
BATCH = 8
QUERIES = 2
KEYS = 4
SLOTS = 3
TILE = 16


def whole(space=pltpu.VMEM):
    return pl.BlockSpec(memory_space=space)


def dot(weights, values):
    return jnp.dot(weights, values, preferred_element_type=f32)


GELU = math.sqrt(2.0 / math.pi)


def gelu(x):
    shaped = x * (GELU + (GELU * 0.044715) * (x * x))
    halved = 0.5 * x
    return halved + halved * jnp.tanh(shaped)


def inside(col, ncols):
    return (col >= 0) & (col < ncols)


def partners(b, k, bands):
    if bands & (bands - 1):
        return lax.rem(b + k, bands), lax.rem(b + bands - k, bands)
    out, bit = 0, 1
    while bit < bands:
        own = lax.rem(lax.div(b, bit), 2)
        out = out + bit * (1 - own if k // bit % 2 else own)
        bit *= 2
    return out, out


def enter(groups_too, sizes):
    nrow, bands, passes, groups = sizes
    g = lax.axis_index("groups")
    p = lax.axis_index("pass")
    b = lax.axis_index("tile") * nrow + lax.axis_index("row")
    barrier = pltpu.get_barrier_semaphore()
    targets = []
    for k in range(1, bands):
        peer = lax.rem(b + k, bands)
        targets.append({"tile": peer // nrow, "row": peer % nrow})
    for dg in range(groups if groups_too else 1):
        for dp in range(passes):
            if (dg, dp) != (0, 0):
                targets.append({"groups": (g + dg) % groups, "pass": (p + dp) % passes})
    for target in targets:
        pl.semaphore_signal(barrier, inc=1, device_id=target, device_id_type=MESH)
    return barrier, len(targets)


def chosen_of(col, cols, ncols, wanted):
    rank = jnp.int32(0)
    chosen = [jnp.int32(0)] * len(wanted)
    for r, offset in enumerate(cols):
        live = inside(col - offset, ncols).astype(jnp.int32)
        for n, k in enumerate(wanted):
            if k <= r:
                chosen[n] = chosen[n] + r * live * (rank == k).astype(jnp.int32)
        rank = rank + live
    return chosen


def roll_rows(x_ref, packed, c, n, r, offset):
    bands, _, _, chans, rows = packed.shape
    lane = lax.broadcasted_iota(jnp.int32, (chans, rows), 1)
    zero = jnp.zeros((chans, rows), f32)
    amount = lax.rem(2 * rows - offset, rows)
    pos = lane + offset
    rolled = [
        pltpu.roll(x_ref[r, c, :, t * rows : (t + 1) * rows].astype(f32), amount, 1)
        for t in range(bands)
    ]
    for t in range(bands):
        low = rolled[t - 1] if t else zero
        high = rolled[t + 1] if t + 1 < bands else zero
        out = jnp.where(pos < 0, low, jnp.where(pos >= rows, high, rolled[t]))
        packed[t, c, n] = out.astype(half)


def exchange(sizes, packed, o_ref, loc, send1, recv1, send2, recv2, between):
    nrow, bands, passes, _ = sizes
    p = lax.axis_index("pass")
    b = lax.axis_index("tile") * nrow + lax.axis_index("row")
    own = pltpu.make_async_copy(packed.at[b], o_ref.at[p, b], loc)
    pending = []

    def forward(src, slot, index):
        for k in range(1, passes):
            copy = pltpu.make_async_remote_copy(
                src_ref=src,
                dst_ref=o_ref.at[p, index],
                send_sem=send2.at[k - 1, slot],
                recv_sem=recv2.at[k - 1, slot],
                device_id={"pass": (p + k) % passes},
                device_id_type=MESH,
            )
            copy.start()
            pending.append(copy)

    forward(packed.at[b], 0, b)
    first = []
    for k in range(1, bands):
        peer, _ = partners(b, k, bands)
        copy = pltpu.make_async_remote_copy(
            src_ref=packed.at[peer],
            dst_ref=o_ref.at[p, b],
            send_sem=send1.at[k - 1],
            recv_sem=recv1.at[k - 1],
            device_id={"tile": peer // nrow, "row": peer % nrow},
            device_id_type=MESH,
        )
        copy.start()
        first.append((k, copy))
    own.start()
    for k, copy in first:
        if between:
            between.pop(0)()
        copy.wait_recv()
        _, source = partners(b, k, bands)
        forward(o_ref.at[p, source], k, source)
    for step in between:
        step()
    for _, copy in first:
        copy.wait_send()
    for copy in pending:
        copy.wait()
    own.wait()


def first_kernel(sizes, cols, *refs):
    hbm, refs = refs[:14], refs[14:]
    o_ref, list_ref, tier, t_qkv, t_out, t_in, t_w1, t_w2, t_gains = refs[:9]
    packed, mine, table, codes, shifts, flags, x_ref, *vmem = refs[9:27]
    loads, move, send, recv, *sems = refs[27:]
    w_query, w_key, w_value, w_out, w_in, w1, w2 = vmem[:7]
    nrow, bands, passes, groups = sizes
    per, own_cols, _, _ = x_ref.shape
    slots, chans, rows = o_ref.shape[3:]
    ncols = own_cols * bands
    g = lax.axis_index("groups")
    p = lax.axis_index("pass")
    b = lax.axis_index("tile") * nrow + lax.axis_index("row")
    peers = [(dg, dp) for dg in range(groups) for dp in range(passes) if (dg, dp) != (0, 0)]
    copies = [
        pltpu.make_async_copy(source, target, loads.at[n])
        for n, (source, target) in enumerate(zip(hbm, [shifts, x_ref, flags, *vmem]))
    ]
    for copy in copies:
        copy.start()
    barrier, greeted = enter(True, sizes)
    copies[0].wait()

    offs = [shifts[1, r] for r in range(per)]
    picked = []
    for c in range(own_cols):
        for n, r in enumerate(chosen_of(b * own_cols + c, offs, ncols, list(range(slots)))):
            picked.append((c, n, r, shifts[0, r]))
    lanes = lax.broadcasted_iota(jnp.int32, (1, mine.shape[1]), 1)
    for r in range(per):
        col = lanes + offs[r]
        slot = jnp.zeros_like(lanes)
        for q in range(r):
            slot = slot + inside(col - offs[q], ncols).astype(jnp.int32)
        live = inside(col, ncols) & (lanes < ncols)
        mine[r : r + 1, :] = jnp.where(live, slot * ncols + col, -1)
    copies[1].wait()
    for c, n, r, offset in picked:
        roll_rows(x_ref, packed, c, n, r, offset)

    pl.semaphore_wait(barrier, greeted)
    metas = [pltpu.make_async_copy(mine, table.at[0, p], move.at[0])]
    metas[0].start()
    for n, (dg, dp) in enumerate(peers):
        copy = pltpu.make_async_remote_copy(
            src_ref=mine,
            dst_ref=table.at[(groups - dg) % groups, p],
            send_sem=send.at[n],
            recv_sem=recv.at[n],
            device_id={"groups": (g + dg) % groups, "pass": (p + dp) % passes},
            device_id_type=MESH,
        )
        copy.start()
        metas.append(copy)

    count = passes * per
    stride = pl.next_power_of_2(cols + 1)
    spots = lax.broadcasted_iota(jnp.int32, (1, list_ref.shape[1]), 1)
    moved = pltpu.make_async_copy(table.at[0], codes, move.at[1])
    filled = dict(
        at=jnp.int32(0),
        rows=[
            jnp.full_like(spots, cols),
            jnp.zeros_like(spots),
            jnp.zeros_like(spots),
            jnp.full_like(spots, 1),
            jnp.zeros_like(spots),
        ],
    )

    def prepare():
        for copy in copies[2:]:
            copy.wait()
        for i, ref in enumerate((w_query, w_key, w_value)):
            t_qkv[i * chans : (i + 1) * chans, :] = ref[...].T
        t_out[...] = w_out[...].T
        t_in[...] = w_in[...].T
        t_w1[...] = w1[...].T
        for i, ref in enumerate(vmem[7:]):
            t_gains[i] = jnp.broadcast_to(ref[...], (rows, chans)).T
        for i in range(w2.shape[0]):
            taps = w2[i].astype(f32)
            for j in range(w2.shape[2]):
                at = (i * w2.shape[2] + j) * chans
                t_w2[:, at : at + chans] = taps[:, j, :].astype(half)

    def gathered():
        for copy in metas:
            copy.wait()
        moved.start()
        most = jnp.max(table[...])
        tier[0] = jnp.maximum(lax.div(most, ncols) + 1 - slots, 0)

    def listed(x):
        def step():
            if x == 0:
                moved.wait()
            token, start, size, below, weight = filled["rows"]
            first = at = filled["at"]
            total = jnp.int32(0)
            for r in range(count):
                code = codes[r // per, r % per, p * cols + x]
                flag = flags[0, r]
                place = (r // per * ncols + lax.rem(code, ncols)) * per + lax.div(code, ncols)
                token = jnp.where(spots == at, (place + 1) * stride + x, token)
                at = at + flag * (code >= 0).astype(jnp.int32)
                total = total + flag
            dead = total - (at - first)
            token = jnp.where(spots == at, x, token)
            here = (spots >= first) & (spots <= at)
            start = jnp.where(here, first, start)
            size = jnp.where(here, at - first, size)
            below = jnp.where(here, dead, below)
            weight = jnp.where(here, jnp.where(spots == at, dead, 1), weight)
            filled["rows"] = [token, start, size, below, weight]
            filled["at"] = at + 1
            if x == cols - 1:
                for n, value in enumerate(filled["rows"]):
                    list_ref[n : n + 1, :] = value
                list_ref[5:6, :] = jnp.full_like(spots, at + 1)
                list_ref[6:7, :] = jnp.full_like(spots, total)

        return step

    steps = [prepare, lambda: None, gathered] + [listed(x) for x in range(cols)]
    exchange(sizes, packed, o_ref, *sems, steps)


def rest_kernel(sizes, skip, s_hbm, x_hbm, o_ref, packed, shifts, x_ref, loads, *sems):
    nrow, bands, _, _ = sizes
    per, own_cols, _, _ = x_ref.shape
    slots = o_ref.shape[3]
    ncols = own_cols * bands
    b = lax.axis_index("tile") * nrow + lax.axis_index("row")
    copies = [
        pltpu.make_async_copy(s_hbm, shifts, loads.at[0]),
        pltpu.make_async_copy(x_hbm, x_ref, loads.at[1]),
    ]
    for copy in copies:
        copy.start()
    barrier, greeted = enter(False, sizes)
    for copy in copies:
        copy.wait()
    offs = [shifts[1, r] for r in range(per)]
    wanted = list(range(skip, skip + slots))
    for c in range(own_cols):
        for n, r in enumerate(chosen_of(b * own_cols + c, offs, ncols, wanted)):
            roll_rows(x_ref, packed, c, n, r, shifts[0, r])
    pl.semaphore_wait(barrier, greeted)
    exchange(sizes, packed, o_ref, *sems, [])


def rms(values, gain):
    mean = jnp.mean(values * values, axis=0, keepdims=True)
    return values * lax.rsqrt(mean + eps) * gain


def join_kernel(cols, per, tokens, *refs):
    gains, w_qkv, w_out, w_in, w_back = refs[:5]
    *pieces, o_ref, edges, q_s, k_s, v_s, mixed_s, total_s = refs[5:]
    held = [ref.shape[1] for ref in pieces]
    chans, rows = pieces[0].shape[2:]
    head = chans // HEADS
    scale = 1.0 / math.sqrt(head)
    stride = pl.next_power_of_2(cols + 1)
    batches = lax.div(tokens[5, 0] + BATCH - 1, BATCH)

    def cell_of(t):
        place = lax.div(tokens[0, t], stride) - 1
        source, slot = lax.div(jnp.maximum(place, 0), per), lax.rem(jnp.maximum(place, 0), per)
        cell = pieces[0][source, jnp.minimum(slot, held[0] - 1)].astype(f32)
        if len(pieces) > 1:
            later = pieces[1][source, jnp.clip(slot - held[0], 0, held[1] - 1)].astype(f32)
            cell = jnp.where(slot < held[0], cell, later)
        return jnp.where(place >= 0, cell, 0.0)

    def part(values, i):
        return values[:, i * rows : (i + 1) * rows]

    def project(j, carry):
        g1, gq, gk = gains[0], gains[1], gains[2]
        normed = [rms(cell_of(j * BATCH + i), g1).astype(half) for i in range(BATCH)]
        qkv = dot(w_qkv[...], jnp.concatenate(normed, axis=1))
        for i in range(BATCH):
            one = part(qkv, i)
            t = j * BATCH + i
            q_s[t] = rms(one[:chans], gq * scale)
            k_s[t] = rms(one[chans : 2 * chans], gk)
            v_s[t] = one[2 * chans :]
        return carry

    lax.fori_loop(0, batches, project, 0)
    total_s[...] = jnp.zeros_like(total_s)

    def attend(j, carry):
        for i0 in range(0, BATCH, QUERIES):
            mine = [j * BATCH + i0 + i for i in range(QUERIES)]
            begin = [tokens[1, t] for t in mine]
            size = [tokens[2, t] for t in mine]
            longest = functools.reduce(jnp.maximum, size)

            def keys_of(group, sums):
                out = []
                for i in range(QUERIES):
                    above, below = sums[i]
                    query = q_s[mine[i]]
                    for u in range(KEYS):
                        k = group * KEYS + u
                        at = begin[i] + jnp.maximum(jnp.minimum(k, size[i] - 1), 0)
                        prod = (query * k_s[at]).reshape(HEADS, head, rows)
                        weight = jnp.exp(jnp.sum(prod, axis=1, keepdims=True))
                        weight = weight * jnp.where(k < size[i], 1.0, 0.0)
                        above = above + weight * v_s[at].reshape(HEADS, head, rows)
                        below = below + weight
                    out.append((above, below))
                return tuple(out)

            init = tuple(
                (
                    jnp.zeros((HEADS, head, rows), f32),
                    jnp.full((HEADS, 1, rows), tokens[3, t].astype(f32), f32),
                )
                for t in mine
            )
            sums = lax.fori_loop(0, lax.div(longest + KEYS - 1, KEYS), keys_of, init)
            for i in range(QUERIES):
                above, below = sums[i]
                mixed = (above * (1.0 / below)).reshape(chans, rows).astype(half)
                mixed_s[:, (i0 + i) * rows : (i0 + i + 1) * rows] = mixed
        back = dot(w_out[...], mixed_s[...])
        g2 = gains[3]
        hidden = [cell_of(j * BATCH + i) + part(back, i) for i in range(BATCH)]
        normed = [rms(one, g2).astype(half) for one in hidden]
        inner = gelu(dot(w_in[...], jnp.concatenate(normed, axis=1)))
        added = dot(w_back[...], inner.astype(half))
        for i in range(BATCH):
            t = j * BATCH + i
            x = lax.rem(tokens[0, t], stride)
            total_s[x] += (hidden[i] + part(added, i)) * tokens[4, t].astype(f32)
        return carry

    lax.fori_loop(0, batches, attend, 0)
    flag_sum = tokens[6, 0].astype(f32)
    folds = chans // TILE
    width = rows // (cols * folds)
    lane = lax.broadcasted_iota(jnp.int32, (TILE, rows), 1)
    top = bottom = jnp.zeros((TILE, rows), f32)
    for x in range(cols):
        joined = total_s[x] / flag_sum
        o_ref[x] = joined.astype(half)
        for f in range(folds):
            piece = joined[f * TILE : (f + 1) * TILE]
            at = (f * cols + x) * width
            here = (lane >= at) & (lane < at + width)
            top = jnp.where(here, pltpu.roll(piece, at, 1), top)
            bottom = jnp.where(here, pltpu.roll(piece, (at + width) % rows, 1), bottom)
    edges[0] = top.astype(half)
    edges[1] = bottom.astype(half)


MOVES = [(dp, db) for dp in (-1, 0, 1) for db in (-1, 0, 1) if (dp, db) != (0, 0)]


def decode_kernel(sizes, j_ref, edges, w1, w2, o_ref, *scratch):
    nrow, bands, passes = sizes
    bufs = scratch[: len(MOVES)]
    taps, acts, send, recv = scratch[len(MOVES) :]
    cols, chans, rows = j_ref.shape
    p = lax.axis_index("pass")
    b = lax.axis_index("tile") * nrow + lax.axis_index("row")

    def exists(dp, db):
        ok = jnp.bool_(True)
        if dp:
            ok = ok & (p + dp >= 0) & (p + dp < passes)
        if db:
            ok = ok & (b + db >= 0) & (b + db < bands)
        return ok

    def target(dp, db):
        k = b + db
        return {"pass": p + dp, "tile": k // nrow, "row": k % nrow}

    barrier = pltpu.get_barrier_semaphore()
    neighbours = jnp.int32(0)
    for dp, db in MOVES:
        there = exists(dp, db)
        neighbours = neighbours + there.astype(jnp.int32)

        @pl.when(there)
        def _():
            pl.semaphore_signal(barrier, inc=1, device_id=target(dp, db), device_id_type=MESH)

    pl.semaphore_wait(barrier, neighbours)

    def copy_of(n):
        dp, db = MOVES[n]
        if db:
            src = edges.at[0 if db < 0 else 1]
        else:
            src = j_ref.at[pl.ds(cols - 2 if dp > 0 else 0, 2)]
        return pltpu.make_async_remote_copy(
            src_ref=src,
            dst_ref=bufs[n],
            send_sem=send.at[n],
            recv_sem=recv.at[n],
            device_id=target(dp, db),
            device_id_type=MESH,
        )

    for n, (dp, db) in enumerate(MOVES):

        @pl.when(exists(dp, db))
        def _():
            copy_of(n).start()

    for n, (dp, db) in enumerate(MOVES):

        @pl.when(exists(-dp, -db))
        def _():
            copy_of(n).wait_recv()

        @pl.when(jnp.logical_not(exists(-dp, -db)))
        def _():
            bufs[n][...] = jnp.zeros_like(bufs[n])

    def side(dp, db):
        return bufs[MOVES.index((-dp, -db))]

    lane = lax.broadcasted_iota(jnp.int32, (chans, rows), 1)
    wide_lane = lax.broadcasted_iota(jnp.int32, (chans, 2 * rows), 1)

    def widen(values):
        last = 2 * rows - 1
        return jnp.concatenate(
            [
                pltpu.roll(values, 1, 1).astype(half),
                values.astype(half),
                pltpu.roll(values, last, 1).astype(half),
            ],
            axis=0,
        )

    folds = chans // TILE
    width = rows // (cols * folds)
    for n in range(cols + 4):
        dp = -1 if n < 2 else (1 if n >= cols + 2 else 0)
        at = n if dp < 0 else (n - cols - 2 if dp > 0 else n - 2)
        middle = j_ref[at] if dp == 0 else side(dp, 0)[at]
        col = cols - 2 + n if dp < 0 else at
        above, below = side(dp, -1)[...].astype(f32), side(dp, 1)[...].astype(f32)
        spots = [(f * cols + col) * width for f in range(folds)]
        after = jnp.concatenate([pltpu.roll(below, (rows - s) % rows, 1) for s in spots], axis=0)
        before = jnp.concatenate([pltpu.roll(above, rows - width - s, 1) for s in spots], axis=0)
        border = jnp.where(lane < rows // 2, after, before)
        taps[n] = widen(jnp.concatenate([middle.astype(f32), border], axis=1))
    row_pos = b * rows + jnp.where(wide_lane < rows + rows // 2, wide_lane, wide_lane - 2 * rows)
    row_inside = (row_pos >= 0) & (row_pos < bands * rows)
    for n in range(cols + 2):
        near = taps[n : n + 3].reshape(9 * chans, 2 * rows)
        act = gelu(dot(w1[...], near))
        col_pos = p * cols + n - 1
        inside = row_inside & (col_pos >= 0) & (col_pos < passes * cols)
        acts[n] = widen(jnp.where(inside, act, 0.0))
    for n in range(cols):
        near = acts[n : n + 3, :, :rows].reshape(9 * chans, rows)
        o_ref[n] = dot(w2[...], near)

    for n, (dp, db) in enumerate(MOVES):

        @pl.when(exists(dp, db))
        def _():
            copy_of(n).wait_send()


def local(
    sizes,
    revisits,
    shifts,
    flags,
    norm1_gain,
    w_query,
    w_key,
    w_value,
    query_gain,
    key_gain,
    w_out,
    norm2_gain,
    w_in,
    w_back,
    conv_first,
    conv_second,
):
    nrow, bands, passes, groups = sizes
    per, own_cols, chans, all_rows = revisits.shape
    rows = all_rows // bands
    ncols = own_cols * bands
    cols = ncols // passes
    count = per * passes
    outs = conv_second.shape[3]
    hidden = w_in.shape[1]
    dma = pltpu.SemaphoreType.DMA
    peers = max(groups * passes - 1, 1)
    shape = jax.ShapeDtypeStruct
    slots = min(SLOTS, per)
    most = cols * (count + 1)
    room = (most + BATCH - 1) // BATCH * BATCH
    width = (most + BATCH + 127) // 128 * 128
    others = max(passes - 1, 1)
    exchange_sems = [dma, dma((bands,)), dma((bands,)), dma((others, bands)), dma((others, bands))]

    def in_hbm(*arrays):
        return [pltpu.with_memory_space_constraint(array, pltpu.HBM) for array in arrays]

    operands = (
        shifts.T,
        revisits,
        flags.T,
        w_query,
        w_key,
        w_value,
        w_out,
        w_in,
        conv_first.reshape(9 * chans, -1),
        conv_second.transpose(0, 3, 1, 2),
        *(gain.reshape(1, chans) for gain in (norm1_gain, query_gain, key_gain, norm2_gain)),
    )
    results = (
        shape((passes, bands, own_cols, slots, chans, rows), half),
        shape((8, width), jnp.int32),
        shape((1,), jnp.int32),
        shape((3 * chans, chans), half),
        shape((chans, chans), half),
        shape((hidden, chans), half),
        shape((chans, 9 * chans), half),
        shape((outs, 9 * chans), half),
        shape((4, chans, rows), f32),
    )
    banded, tokens, tier, t_qkv, t_out, t_in, t_w1, t_w2, gains = pl.pallas_call(
        functools.partial(first_kernel, sizes, cols),
        out_shape=results,
        in_specs=[whole(pltpu.HBM)] * len(operands),
        out_specs=tuple(whole(pltpu.SMEM) if n == 2 else whole() for n in range(len(results))),
        scratch_shapes=[
            pltpu.VMEM((bands, own_cols, slots, chans, rows), half),
            pltpu.VMEM((per, 128), jnp.int32),
            pltpu.VMEM((groups, passes, per, 128), jnp.int32),
            pltpu.SMEM((passes, per, 128), jnp.int32),
            pltpu.SMEM((2, per), jnp.int32),
            pltpu.SMEM((1, count), jnp.int32),
            pltpu.VMEM(revisits.shape, half),
            *(pltpu.VMEM(array.shape, array.dtype) for array in operands[3:]),
            dma((len(operands),)),
            dma((2,)),
            dma((peers,)),
            dma((peers,)),
            *exchange_sems,
        ],
        compiler_params=pltpu.CompilerParams(
            collective_id=0, has_side_effects=True, vmem_limit_bytes=16 * MIB
        ),
        name="first",
    )(*in_hbm(*operands))

    def join(tokens, weights, *pieces):
        return pl.pallas_call(
            functools.partial(join_kernel, cols, per),
            out_shape=(shape((cols, chans, rows), half), shape((2, TILE, rows), half)),
            in_specs=[whole(pltpu.SMEM)] + [whole()] * (len(weights) + len(pieces)),
            out_specs=(whole(), whole()),
            scratch_shapes=[
                pltpu.VMEM((room, chans, rows), f32),
                pltpu.VMEM((room, chans, rows), f32),
                pltpu.VMEM((room, chans, rows), f32),
                pltpu.VMEM((chans, BATCH * rows), half),
                pltpu.VMEM((cols + 1, chans, rows), f32),
            ],
            compiler_params=pltpu.CompilerParams(vmem_limit_bytes=20 * MIB),
            name="join",
        )(tokens, *weights, *(ref.reshape(passes * ncols, -1, chans, rows) for ref in pieces))

    def branch(more):
        def run(tokens, weights, banded, shifts, revisits):
            if not more:
                return join(tokens, weights, banded)
            rest = pl.pallas_call(
                functools.partial(rest_kernel, sizes, slots),
                out_shape=shape((passes, bands, own_cols, more, chans, rows), half),
                in_specs=[whole(pltpu.HBM)] * 2,
                out_specs=whole(),
                scratch_shapes=[
                    pltpu.VMEM((bands, own_cols, more, chans, rows), half),
                    pltpu.SMEM((2, per), jnp.int32),
                    pltpu.VMEM(revisits.shape, half),
                    dma((2,)),
                    *exchange_sems,
                ],
                compiler_params=pltpu.CompilerParams(
                    collective_id=1 + more, has_side_effects=True, vmem_limit_bytes=16 * MIB
                ),
                name="rest",
            )(*in_hbm(shifts, revisits))
            return join(tokens, weights, banded, rest)

        return run

    weights = (gains, t_qkv, t_out, t_in, w_back.T)
    given = (tokens, weights, banded, shifts.T, revisits)
    if per > slots:
        branches = [branch(more) for more in range(per - slots + 1)]
        joined, edges = lax.switch(tier[0], branches, *given)
    else:
        joined, edges = branch(0)(*given)
    return pl.pallas_call(
        functools.partial(decode_kernel, sizes[:3]),
        out_shape=shape((cols, outs, rows), f32),
        in_specs=[whole()] * 4,
        out_specs=whole(),
        scratch_shapes=[
            pltpu.VMEM((TILE, rows) if db else (2, chans, rows), half) for dp, db in MOVES
        ]
        + [
            pltpu.VMEM((cols + 4, 3 * chans, 2 * rows), half),
            pltpu.VMEM((cols + 2, 3 * chans, 2 * rows), half),
            dma((len(MOVES),)),
            dma((len(MOVES),)),
        ],
        compiler_params=pltpu.CompilerParams(
            collective_id=1, has_side_effects=True, vmem_limit_bytes=16 * MIB
        ),
        name="decode",
    )(joined, edges, t_w1, t_w2)


def solution(mesh):
    shape = mesh.shape
    sizes = (shape["row"], shape["tile"] * shape["row"], shape["pass"], shape["groups"])
    fixed = [P()] * 12
    return jax.shard_map(
        functools.partial(local, sizes),
        mesh=mesh,
        in_specs=(
            P(("groups", "pass"), ("tile", "row"), None, None),
            P(("groups", "pass"), None),
            P("groups", ("tile", "row")),
            *fixed,
        ),
        out_specs=P(("groups", "pass"), None, ("tile", "row")),
        check_vma=False,
    )
```

```python
import functools
import math

import jax
import jax.numpy as jnp
import numpy as np
from jax import lax
from jax.experimental import pallas as pl
from jax.experimental.pallas import tpu as pltpu
from jax.sharding import PartitionSpec as P

HEADS = 4
eps = 1e-05
f32 = jnp.float32
half = jnp.bfloat16
MESH = pl.DeviceIdType.MESH
MIB = 1024 * 1024
PROJECT = 8
BATCH = 10
QUERIES = 2
KEYS = 4
SLOTS = 3
TILE = 16


def whole(space=pltpu.VMEM):
    return pl.BlockSpec(memory_space=space)


def dot(weights, values):
    return jnp.dot(weights, values, preferred_element_type=f32)


GELU = math.sqrt(2.0 / math.pi)


def gelu(x):
    shaped = x * (GELU + (GELU * 0.044715) * (x * x))
    halved = 0.5 * x
    return halved + halved * jnp.tanh(shaped)


def inside(col, ncols):
    return (col >= 0) & (col < ncols)


def partners(b, k, bands):
    if bands & (bands - 1):
        return lax.rem(b + k, bands), lax.rem(b + bands - k, bands)
    out, bit = 0, 1
    while bit < bands:
        own = lax.rem(lax.div(b, bit), 2)
        out = out + bit * (1 - own if k // bit % 2 else own)
        bit *= 2
    return out, out


def widths(count):
    return [width for width in (2, 3, 4, 5, 6, 8) if width < count] + [count]


def enter(groups_too, sizes):
    nrow, bands, passes, groups = sizes
    g = lax.axis_index("groups")
    p = lax.axis_index("pass")
    b = lax.axis_index("tile") * nrow + lax.axis_index("row")
    barrier = pltpu.get_barrier_semaphore()
    targets = []
    for k in range(1, bands):
        peer = lax.rem(b + k, bands)
        targets.append({"tile": peer // nrow, "row": peer % nrow})
    for dg in range(groups if groups_too else 1):
        for dp in range(passes):
            if (dg, dp) != (0, 0):
                targets.append({"groups": (g + dg) % groups, "pass": (p + dp) % passes})
    for target in targets:
        pl.semaphore_signal(barrier, inc=1, device_id=target, device_id_type=MESH)
    return barrier, len(targets)


def chosen_of(col, cols, ncols, wanted):
    rank = jnp.int32(0)
    chosen = [jnp.int32(0)] * len(wanted)
    for r, offset in enumerate(cols):
        live = inside(col - offset, ncols).astype(jnp.int32)
        for n, k in enumerate(wanted):
            if k <= r:
                chosen[n] = chosen[n] + r * live * (rank == k).astype(jnp.int32)
        rank = rank + live
    return chosen


def roll_rows(x_ref, packed, c, n, r, offset):
    bands, _, _, chans, rows = packed.shape
    lane = lax.broadcasted_iota(jnp.int32, (chans, rows), 1)
    zero = jnp.zeros((chans, rows), f32)
    amount = lax.rem(2 * rows - offset, rows)
    pos = lane + offset
    rolled = [
        pltpu.roll(x_ref[r, c, :, t * rows : (t + 1) * rows].astype(f32), amount, 1)
        for t in range(bands)
    ]
    for t in range(bands):
        low = rolled[t - 1] if t else zero
        high = rolled[t + 1] if t + 1 < bands else zero
        out = jnp.where(pos < 0, low, jnp.where(pos >= rows, high, rolled[t]))
        packed[t, c, n] = out.astype(half)


def exchange(sizes, packed, o_ref, loc, send1, recv1, send2, recv2, between):
    nrow, bands, passes, _ = sizes
    p = lax.axis_index("pass")
    b = lax.axis_index("tile") * nrow + lax.axis_index("row")
    own = pltpu.make_async_copy(packed.at[b], o_ref.at[p, b], loc)
    pending = []

    def forward(src, slot, index):
        for k in range(1, passes):
            copy = pltpu.make_async_remote_copy(
                src_ref=src,
                dst_ref=o_ref.at[p, index],
                send_sem=send2.at[k - 1, slot],
                recv_sem=recv2.at[k - 1, slot],
                device_id={"pass": (p + k) % passes},
                device_id_type=MESH,
            )
            copy.start()
            pending.append(copy)

    forward(packed.at[b], 0, b)
    first = []
    for k in range(1, bands):
        peer, _ = partners(b, k, bands)
        copy = pltpu.make_async_remote_copy(
            src_ref=packed.at[peer],
            dst_ref=o_ref.at[p, b],
            send_sem=send1.at[k - 1],
            recv_sem=recv1.at[k - 1],
            device_id={"tile": peer // nrow, "row": peer % nrow},
            device_id_type=MESH,
        )
        copy.start()
        first.append((k, copy))
    own.start()
    for k, copy in first:
        if between:
            between.pop(0)()
        copy.wait_recv()
        _, source = partners(b, k, bands)
        forward(o_ref.at[p, source], k, source)
    for step in between:
        step()
    for _, copy in first:
        copy.wait_send()
    for copy in pending:
        copy.wait()
    own.wait()


def first_kernel(sizes, cols, *refs):
    hbm, refs = refs[:14], refs[14:]
    o_ref, list_ref, which, t_qkv, t_out, t_in, t_w1, t_w2, t_gains = refs[:9]
    packed, mine, table, codes, shifts, flags, x_ref, *vmem = refs[9:27]
    loads, move, send, recv, *sems = refs[27:]
    w_query, w_key, w_value, w_out, w_in, w1, w2 = vmem[:7]
    nrow, bands, passes, groups = sizes
    per, own_cols, _, _ = x_ref.shape
    slots, chans, rows = o_ref.shape[3:]
    ncols = own_cols * bands
    g = lax.axis_index("groups")
    p = lax.axis_index("pass")
    b = lax.axis_index("tile") * nrow + lax.axis_index("row")
    peers = [(dg, dp) for dg in range(groups) for dp in range(passes) if (dg, dp) != (0, 0)]
    copies = [
        pltpu.make_async_copy(source, target, loads.at[n])
        for n, (source, target) in enumerate(zip(hbm, [shifts, x_ref, flags, *vmem]))
    ]
    for copy in copies:
        copy.start()
    barrier, greeted = enter(True, sizes)
    copies[0].wait()

    offs = [shifts[1, r] for r in range(per)]
    picked = []
    for c in range(own_cols):
        for n, r in enumerate(chosen_of(b * own_cols + c, offs, ncols, list(range(slots)))):
            picked.append((c, n, r, shifts[0, r]))
    lanes = lax.broadcasted_iota(jnp.int32, (1, mine.shape[1]), 1)
    for r in range(per):
        col = lanes + offs[r]
        slot = jnp.zeros_like(lanes)
        for q in range(r):
            slot = slot + inside(col - offs[q], ncols).astype(jnp.int32)
        live = inside(col, ncols) & (lanes < ncols)
        mine[r : r + 1, :] = jnp.where(live, slot * ncols + col, -1)
    copies[1].wait()
    for c, n, r, offset in picked:
        roll_rows(x_ref, packed, c, n, r, offset)

    pl.semaphore_wait(barrier, greeted)
    metas = [pltpu.make_async_copy(mine, table.at[0, p], move.at[0])]
    metas[0].start()
    for n, (dg, dp) in enumerate(peers):
        copy = pltpu.make_async_remote_copy(
            src_ref=mine,
            dst_ref=table.at[(groups - dg) % groups, p],
            send_sem=send.at[n],
            recv_sem=recv.at[n],
            device_id={"groups": (g + dg) % groups, "pass": (p + dp) % passes},
            device_id_type=MESH,
        )
        copy.start()
        metas.append(copy)

    count = passes * per
    spots = lax.broadcasted_iota(jnp.int32, (1, list_ref.shape[1]), 1)
    moved = pltpu.make_async_copy(table.at[0], codes, move.at[1])
    sizes_of = [jnp.zeros_like(spots)]

    def prepare():
        for copy in copies[2:]:
            copy.wait()
        for i, ref in enumerate((w_query, w_key, w_value)):
            t_qkv[i * chans : (i + 1) * chans, :] = ref[...].T
        t_out[...] = w_out[...].T
        t_in[...] = w_in[...].T
        t_w1[...] = w1[...].T
        for i, ref in enumerate(vmem[7:]):
            t_gains[i] = jnp.broadcast_to(ref[...], (rows, chans)).T
        for i in range(w2.shape[0]):
            taps = w2[i].astype(f32)
            for j in range(w2.shape[2]):
                at = (i * w2.shape[2] + j) * chans
                t_w2[:, at : at + chans] = taps[:, j, :].astype(half)

    def gathered():
        for copy in metas:
            copy.wait()
        moved.start()
        held = table[...]
        alive = [
            sum((held[i, j] >= 0).astype(jnp.int32).sum(axis=0) for j in range(passes))
            for i in range(groups)
        ]
        busiest = jnp.max(functools.reduce(jnp.maximum, alive))
        more = lax.div(jnp.max(held), ncols) + 1 - slots
        plain = sum((busiest > width).astype(jnp.int32) for width in widths(count)[:-1])
        if per > slots:
            late = len(widths(count)) + jnp.where(
                more > 1, 2, jnp.where(busiest > widths(count)[-3], 1, 0)
            )
            plain = jnp.where(more > 0, late, plain)
        which[0] = plain

    def listed(x):
        def step():
            if x == 0:
                moved.wait()
            token = jnp.zeros_like(spots)
            at = jnp.int32(0)
            total = jnp.int32(0)
            for r in range(count):
                code = codes[r // per, r % per, p * cols + x]
                flag = flags[0, r]
                live = flag * (code >= 0).astype(jnp.int32)
                place = (r // per * ncols + lax.rem(code, ncols)) * per + lax.div(code, ncols)
                token = jnp.where(spots == at, (place + 1) * live, token)
                at = at + live
                total = total + flag
            list_ref[x : x + 1, :] = token
            sizes_of[0] = jnp.where(spots == x, at, sizes_of[0])
            if x == cols - 1:
                list_ref[cols : cols + 1, :] = jnp.zeros_like(spots)
                list_ref[cols + 1 : cols + 2, :] = jnp.where(spots == cols + 1, total, sizes_of[0])

        return step

    steps = [prepare, lambda: None, gathered] + [listed(x) for x in range(cols)]
    exchange(sizes, packed, o_ref, *sems, steps)


def rest_kernel(sizes, skip, s_hbm, x_hbm, o_ref, packed, shifts, x_ref, loads, *sems):
    nrow, bands, _, _ = sizes
    per, own_cols, _, _ = x_ref.shape
    slots = o_ref.shape[3]
    ncols = own_cols * bands
    b = lax.axis_index("tile") * nrow + lax.axis_index("row")
    copies = [
        pltpu.make_async_copy(s_hbm, shifts, loads.at[0]),
        pltpu.make_async_copy(x_hbm, x_ref, loads.at[1]),
    ]
    for copy in copies:
        copy.start()
    barrier, greeted = enter(False, sizes)
    for copy in copies:
        copy.wait()
    offs = [shifts[1, r] for r in range(per)]
    wanted = list(range(skip, skip + slots))
    for c in range(own_cols):
        for n, r in enumerate(chosen_of(b * own_cols + c, offs, ncols, wanted)):
            roll_rows(x_ref, packed, c, n, r, shifts[0, r])
    pl.semaphore_wait(barrier, greeted)
    exchange(sizes, packed, o_ref, *sems, [])


def rms(values, gain):
    mean = jnp.mean(values * values, axis=0, keepdims=True)
    return values * lax.rsqrt(mean + eps) * gain


MOVES = [(dp, db) for dp in (-1, 0, 1) for db in (-1, 0, 1) if (dp, db) != (0, 0)]


def cut(total, most):
    batches = -(-total // most)
    return batches, -(-total // batches)


def finish_kernel(sizes, per, width, *refs):
    tokens, gains, w_qkv, w_out, w_in, w_back, w1, w2 = refs[:8]
    *pieces, o_ref, q_s, k_s, v_s, mixed_s, total_s, j_ref, edges = refs[8 : -len(MOVES) - 4]
    bufs = refs[-len(MOVES) - 4 : -4]
    taps, acts, send, recv = refs[-4:]
    nrow, bands, passes = sizes
    cols, chans, rows = j_ref.shape
    head = chans // HEADS
    scale = 1.0 / math.sqrt(head)
    held = [ref.shape[1] for ref in pieces]
    p = lax.axis_index("pass")
    b = lax.axis_index("tile") * nrow + lax.axis_index("row")

    def exists(dp, db):
        ok = jnp.bool_(True)
        if dp:
            ok = ok & (p + dp >= 0) & (p + dp < passes)
        if db:
            ok = ok & (b + db >= 0) & (b + db < bands)
        return ok

    def target(dp, db):
        k = b + db
        return {"pass": p + dp, "tile": k // nrow, "row": k % nrow}

    barrier = pltpu.get_barrier_semaphore()
    neighbours = jnp.int32(0)
    for dp, db in MOVES:
        there = exists(dp, db)
        neighbours = neighbours + there.astype(jnp.int32)

        @pl.when(there)
        def _():
            pl.semaphore_signal(barrier, inc=1, device_id=target(dp, db), device_id_type=MESH)

    flag_sum = tokens[cols + 1, cols + 1].astype(f32)

    def cell_of(x, j):
        code = tokens[x, j]
        place = jnp.maximum(code - 1, 0)
        source, slot = lax.div(place, per), lax.rem(place, per)
        cell = pieces[0][source, jnp.minimum(slot, held[0] - 1)].astype(f32)
        if len(pieces) > 1:
            later = pieces[1][source, jnp.clip(slot - held[0], 0, held[1] - 1)].astype(f32)
            cell = jnp.where(slot < held[0], cell, later)
        return jnp.where(code > 0, cell, 0.0)

    def part(values, i):
        return values[:, i * rows : (i + 1) * rows]

    batches, batch = cut(cols * width, PROJECT)

    def project(n, carry):
        g1, gq, gk = gains[0], gains[1], gains[2]
        places = [n * batch + i for i in range(batch)]
        normed = [
            rms(cell_of(lax.div(t, width), lax.rem(t, width)), g1).astype(half) for t in places
        ]
        qkv = dot(w_qkv[...], jnp.concatenate(normed, axis=1))
        for i, t in enumerate(places):
            one = part(qkv, i)
            q_s[t] = rms(one[:chans], gq * scale)
            k_s[t] = rms(one[chans : 2 * chans], gk)
            v_s[t] = one[2 * chans :]
        return carry

    lax.fori_loop(0, batches, project, 0)
    short = width <= 6

    def column(x, carry):
        size = tokens[cols + 1, x]
        dead = flag_sum - size.astype(f32)
        base = x * width

        def keys_of(queries, keys, sums):
            out = []
            for query, (above, below) in zip(queries, sums):
                q = q_s[base + query]
                for k in keys:
                    prod = (q * k_s[base + k]).reshape(HEADS, head, rows)
                    weight = jnp.exp(jnp.sum(prod, axis=1, keepdims=True))
                    weight = weight * jnp.where(k < size, 1.0, 0.0)
                    above = above + weight * v_s[base + k].reshape(HEADS, head, rows)
                    below = below + weight
                out.append((above, below))
            return tuple(out)

        def attend(queries):
            sums = tuple(
                (jnp.zeros((HEADS, head, rows), f32), jnp.full((HEADS, 1, rows), dead, f32))
                for _ in queries
            )
            if short:
                sums = keys_of(queries, range(width), sums)
            else:
                sums = lax.fori_loop(
                    0,
                    width // KEYS,
                    lambda n, sums: keys_of(queries, [n * KEYS + u for u in range(KEYS)], sums),
                    sums,
                )
            for query, (above, below) in zip(queries, sums):
                mixed = (above * (1.0 / below)).reshape(chans, rows)
                mixed_s[x * (width + 1) + query] = mixed.astype(half)

        if short:
            for query in range(0, width, QUERIES):
                attend(list(range(query, min(query + QUERIES, width))))
        else:

            def some(n, carry):
                attend([n * QUERIES + i for i in range(QUERIES)])
                return carry

            lax.fori_loop(0, width // QUERIES, some, 0)
        if short:
            shared = jnp.zeros((chans, rows), f32)
            for k in range(width):
                shared = shared + v_s[base + k]
        else:
            shared = lax.fori_loop(
                0, width, lambda k, total: total + v_s[base + k], jnp.zeros((chans, rows), f32)
            )
        mixed_s[x * (width + 1) + width] = (shared / flag_sum).astype(half)
        return carry

    lax.fori_loop(0, cols, column, 0)
    total_s[...] = jnp.zeros_like(total_s)
    steps, step = cut(cols * (width + 1), BATCH)

    def feed(n, carry):
        places = [n * step + i for i in range(step)]
        where = [(lax.div(t, width + 1), lax.rem(t, width + 1)) for t in places]
        back = dot(w_out[...], jnp.concatenate([mixed_s[t] for t in places], axis=1))
        g2 = gains[3]
        hidden = [cell_of(*at) + part(back, i) for i, at in enumerate(where)]
        normed = [rms(one, g2).astype(half) for one in hidden]
        inner = gelu(dot(w_in[...], jnp.concatenate(normed, axis=1)))
        added = dot(w_back[...], inner.astype(half))
        for i, (x, j) in enumerate(where):
            size = tokens[cols + 1, x]
            dead = flag_sum - size.astype(f32)
            weight = jnp.where(j < size, 1.0, jnp.where(j == width, dead, 0.0))
            total_s[x] += (hidden[i] + part(added, i)) * weight
        return carry

    lax.fori_loop(0, steps, feed, 0)
    folds = chans // TILE
    strip = rows // (cols * folds)
    fold_lane = lax.broadcasted_iota(jnp.int32, (TILE, rows), 1)
    top = bottom = jnp.zeros((TILE, rows), f32)
    for x in range(cols):
        joined = total_s[x] / flag_sum
        j_ref[x] = joined.astype(half)
        for f in range(folds):
            piece = joined[f * TILE : (f + 1) * TILE]
            at = (f * cols + x) * strip
            here = (fold_lane >= at) & (fold_lane < at + strip)
            top = jnp.where(here, pltpu.roll(piece, at, 1), top)
            bottom = jnp.where(here, pltpu.roll(piece, (at + strip) % rows, 1), bottom)
    edges[0] = top.astype(half)
    edges[1] = bottom.astype(half)

    pl.semaphore_wait(barrier, neighbours)

    def copy_of(n):
        dp, db = MOVES[n]
        if db:
            src = edges.at[0 if db < 0 else 1]
        else:
            src = j_ref.at[pl.ds(cols - 2 if dp > 0 else 0, 2)]
        return pltpu.make_async_remote_copy(
            src_ref=src,
            dst_ref=bufs[n],
            send_sem=send.at[n],
            recv_sem=recv.at[n],
            device_id=target(dp, db),
            device_id_type=MESH,
        )

    for n, (dp, db) in enumerate(MOVES):

        @pl.when(exists(dp, db))
        def _():
            copy_of(n).start()

    for n, (dp, db) in enumerate(MOVES):

        @pl.when(exists(-dp, -db))
        def _():
            copy_of(n).wait_recv()

        @pl.when(jnp.logical_not(exists(-dp, -db)))
        def _():
            bufs[n][...] = jnp.zeros_like(bufs[n])

    def side(dp, db):
        return bufs[MOVES.index((-dp, -db))]

    lane = lax.broadcasted_iota(jnp.int32, (chans, rows), 1)
    wide_lane = lax.broadcasted_iota(jnp.int32, (chans, 2 * rows), 1)

    def widen(values):
        last = 2 * rows - 1
        return jnp.concatenate(
            [
                pltpu.roll(values, 1, 1).astype(half),
                values.astype(half),
                pltpu.roll(values, last, 1).astype(half),
            ],
            axis=0,
        )

    for n in range(cols + 4):
        dp = -1 if n < 2 else (1 if n >= cols + 2 else 0)
        at = n if dp < 0 else (n - cols - 2 if dp > 0 else n - 2)
        middle = j_ref[at] if dp == 0 else side(dp, 0)[at]
        col = cols - 2 + n if dp < 0 else at
        above, below = side(dp, -1)[...].astype(f32), side(dp, 1)[...].astype(f32)
        spots = [(f * cols + col) * strip for f in range(folds)]
        after = jnp.concatenate([pltpu.roll(below, (rows - s) % rows, 1) for s in spots], axis=0)
        before = jnp.concatenate([pltpu.roll(above, rows - strip - s, 1) for s in spots], axis=0)
        border = jnp.where(lane < rows // 2, after, before)
        taps[n] = widen(jnp.concatenate([middle.astype(f32), border], axis=1))
    row_pos = b * rows + jnp.where(wide_lane < rows + rows // 2, wide_lane, wide_lane - 2 * rows)
    row_inside = (row_pos >= 0) & (row_pos < bands * rows)
    for n in range(cols + 2):
        near = taps[n : n + 3].reshape(9 * chans, 2 * rows)
        act = gelu(dot(w1[...], near))
        col_pos = p * cols + n - 1
        inside = row_inside & (col_pos >= 0) & (col_pos < passes * cols)
        acts[n] = widen(jnp.where(inside, act, 0.0))
    for n in range(cols):
        near = acts[n : n + 3, :, :rows].reshape(9 * chans, rows)
        o_ref[n] = dot(w2[...], near)

    for n, (dp, db) in enumerate(MOVES):

        @pl.when(exists(dp, db))
        def _():
            copy_of(n).wait_send()


def local(
    sizes,
    revisits,
    shifts,
    flags,
    norm1_gain,
    w_query,
    w_key,
    w_value,
    query_gain,
    key_gain,
    w_out,
    norm2_gain,
    w_in,
    w_back,
    conv_first,
    conv_second,
):
    nrow, bands, passes, groups = sizes
    per, own_cols, chans, all_rows = revisits.shape
    rows = all_rows // bands
    ncols = own_cols * bands
    cols = ncols // passes
    count = per * passes
    outs = conv_second.shape[3]
    hidden = w_in.shape[1]
    dma = pltpu.SemaphoreType.DMA
    peers = max(groups * passes - 1, 1)
    shape = jax.ShapeDtypeStruct
    slots = min(SLOTS, per)
    others = max(passes - 1, 1)
    exchange_sems = [dma, dma((bands,)), dma((bands,)), dma((others, bands)), dma((others, bands))]

    def in_hbm(*arrays):
        return [pltpu.with_memory_space_constraint(array, pltpu.HBM) for array in arrays]

    operands = (
        shifts.T,
        revisits,
        flags.T,
        w_query,
        w_key,
        w_value,
        w_out,
        w_in,
        conv_first.reshape(9 * chans, -1),
        conv_second.transpose(0, 3, 1, 2),
        *(gain.reshape(1, chans) for gain in (norm1_gain, query_gain, key_gain, norm2_gain)),
    )
    results = (
        shape((passes, bands, own_cols, slots, chans, rows), half),
        shape(((cols + 2 + 7) // 8 * 8, 128), jnp.int32),
        shape((1,), jnp.int32),
        shape((3 * chans, chans), half),
        shape((chans, chans), half),
        shape((hidden, chans), half),
        shape((chans, 9 * chans), half),
        shape((outs, 9 * chans), half),
        shape((4, chans, rows), f32),
    )
    banded, tokens, which, t_qkv, t_out, t_in, t_w1, t_w2, gains = pl.pallas_call(
        functools.partial(first_kernel, sizes, cols),
        out_shape=results,
        in_specs=[whole(pltpu.HBM)] * len(operands),
        out_specs=tuple(whole(pltpu.SMEM) if n == 2 else whole() for n in range(len(results))),
        scratch_shapes=[
            pltpu.VMEM((bands, own_cols, slots, chans, rows), half),
            pltpu.VMEM((per, 128), jnp.int32),
            pltpu.VMEM((groups, passes, per, 128), jnp.int32),
            pltpu.SMEM((passes, per, 128), jnp.int32),
            pltpu.SMEM((2, per), jnp.int32),
            pltpu.SMEM((1, count), jnp.int32),
            pltpu.VMEM(revisits.shape, half),
            *(pltpu.VMEM(array.shape, array.dtype) for array in operands[3:]),
            dma((len(operands),)),
            dma((2,)),
            dma((peers,)),
            dma((peers,)),
            *exchange_sems,
        ],
        compiler_params=pltpu.CompilerParams(
            collective_id=0, has_side_effects=True, vmem_limit_bytes=16 * MIB
        ),
        name="first",
    )(*in_hbm(*operands))

    def finish(width, identity, tokens, weights, *pieces):
        batches, batch = cut(cols * width, PROJECT)
        steps, step = cut(cols * (width + 1), BATCH)
        return pl.pallas_call(
            functools.partial(finish_kernel, sizes[:3], per, width),
            out_shape=shape((cols, outs, rows), f32),
            in_specs=[whole(pltpu.SMEM)] + [whole()] * (len(weights) + len(pieces)),
            out_specs=whole(),
            scratch_shapes=[
                pltpu.VMEM((batches * batch, chans, rows), f32),
                pltpu.VMEM((batches * batch, chans, rows), f32),
                pltpu.VMEM((batches * batch, chans, rows), f32),
                pltpu.VMEM((steps * step, chans, rows), half),
                pltpu.VMEM((cols + 1, chans, rows), f32),
                pltpu.VMEM((cols, chans, rows), half),
                pltpu.VMEM((2, TILE, rows), half),
                *(
                    pltpu.VMEM((TILE, rows) if db else (2, chans, rows), half)
                    for dp, db in MOVES
                ),
                pltpu.VMEM((cols + 4, 3 * chans, 2 * rows), half),
                pltpu.VMEM((cols + 2, 3 * chans, 2 * rows), half),
                dma((len(MOVES),)),
                dma((len(MOVES),)),
            ],
            compiler_params=pltpu.CompilerParams(
                collective_id=identity, has_side_effects=True, vmem_limit_bytes=24 * MIB
            ),
            name="finish",
        )(tokens, *weights, *(ref.reshape(passes * ncols, -1, chans, rows) for ref in pieces))

    def branch(n, more, width):
        def run(tokens, weights, banded, shifts, revisits):
            if not more:
                return finish(width, 1 + 2 * n, tokens, weights, banded)
            rest = pl.pallas_call(
                functools.partial(rest_kernel, sizes, slots),
                out_shape=shape((passes, bands, own_cols, more, chans, rows), half),
                in_specs=[whole(pltpu.HBM)] * 2,
                out_specs=whole(),
                scratch_shapes=[
                    pltpu.VMEM((bands, own_cols, more, chans, rows), half),
                    pltpu.SMEM((2, per), jnp.int32),
                    pltpu.VMEM(revisits.shape, half),
                    dma((2,)),
                    *exchange_sems,
                ],
                compiler_params=pltpu.CompilerParams(
                    collective_id=2 + 2 * n, has_side_effects=True, vmem_limit_bytes=16 * MIB
                ),
                name="rest",
            )(*in_hbm(shifts, revisits))
            return finish(width, 1 + 2 * n, tokens, weights, banded, rest)

        return run

    weights = (gains, t_qkv, t_out, t_in, w_back.T, t_w1, t_w2)
    plans = [(0, width) for width in widths(count)]
    if per > slots:
        plans += [(1, widths(count)[-3]), (1, count), (per - slots, count)]
    branches = [branch(n, *plan) for n, plan in enumerate(plans)]
    return lax.switch(which[0], branches, tokens, weights, banded, shifts.T, revisits)


def solution(mesh):
    shape = mesh.shape
    sizes = (shape["row"], shape["tile"] * shape["row"], shape["pass"], shape["groups"])
    fixed = [P()] * 12
    return jax.shard_map(
        functools.partial(local, sizes),
        mesh=mesh,
        in_specs=(
            P(("groups", "pass"), ("tile", "row"), None, None),
            P(("groups", "pass"), None),
            P("groups", ("tile", "row")),
            *fixed,
        ),
        out_specs=P(("groups", "pass"), None, ("tile", "row")),
        check_vma=False,
    )
```

```python
import functools
import math

import jax
import jax.numpy as jnp
import numpy as np
from jax import lax
from jax.experimental import pallas as pl
from jax.experimental.pallas import tpu as pltpu
from jax.sharding import PartitionSpec as P

HEADS = 4
eps = 1e-05
f32 = jnp.float32
half = jnp.bfloat16
MESH = pl.DeviceIdType.MESH
MIB = 1024 * 1024
PROJECT = 8
BATCH = 10
QUERIES = 2
KEYS = 4
SLOTS = 3
TILE = 16


def whole(space=pltpu.VMEM):
    return pl.BlockSpec(memory_space=space)


def dot(weights, values):
    return jnp.dot(weights, values, preferred_element_type=f32)


GELU = math.sqrt(2.0 / math.pi)


def gelu(x):
    shaped = x * (GELU + (GELU * 0.044715) * (x * x))
    halved = 0.5 * x
    return halved + halved * jnp.tanh(shaped)


def inside(col, ncols):
    return (col >= 0) & (col < ncols)


def partners(b, k, bands):
    if bands & (bands - 1):
        return lax.rem(b + k, bands), lax.rem(b + bands - k, bands)
    out, bit = 0, 1
    while bit < bands:
        own = lax.rem(lax.div(b, bit), 2)
        out = out + bit * (1 - own if k // bit % 2 else own)
        bit *= 2
    return out, out


def widths(count):
    return [width for width in (2, 3, 4, 5, 6, 8) if width < count] + [count]


def enter(groups_too, sizes):
    nrow, bands, passes, groups = sizes
    g = lax.axis_index("groups")
    p = lax.axis_index("pass")
    b = lax.axis_index("tile") * nrow + lax.axis_index("row")
    barrier = pltpu.get_barrier_semaphore()
    targets = []
    for k in range(1, bands):
        peer = lax.rem(b + k, bands)
        targets.append({"tile": peer // nrow, "row": peer % nrow})
    for dg in range(groups if groups_too else 1):
        for dp in range(passes):
            if (dg, dp) != (0, 0):
                targets.append({"groups": (g + dg) % groups, "pass": (p + dp) % passes})
    for target in targets:
        pl.semaphore_signal(barrier, inc=1, device_id=target, device_id_type=MESH)
    return barrier, len(targets)


def chosen_of(col, cols, ncols, wanted):
    rank = jnp.int32(0)
    chosen = [jnp.int32(0)] * len(wanted)
    for r, offset in enumerate(cols):
        live = inside(col - offset, ncols).astype(jnp.int32)
        for n, k in enumerate(wanted):
            if k <= r:
                chosen[n] = chosen[n] + r * live * (rank == k).astype(jnp.int32)
        rank = rank + live
    return chosen


def roll_rows(x_ref, packed, c, n, r, offset):
    bands, _, _, chans, rows = packed.shape
    lane = lax.broadcasted_iota(jnp.int32, (chans, rows), 1)
    zero = jnp.zeros((chans, rows), f32)
    amount = lax.rem(2 * rows - offset, rows)
    pos = lane + offset
    rolled = [
        pltpu.roll(x_ref[r, c, :, t * rows : (t + 1) * rows].astype(f32), amount, 1)
        for t in range(bands)
    ]
    for t in range(bands):
        low = rolled[t - 1] if t else zero
        high = rolled[t + 1] if t + 1 < bands else zero
        out = jnp.where(pos < 0, low, jnp.where(pos >= rows, high, rolled[t]))
        packed[t, c, n] = out.astype(half)


def exchange(sizes, packed, o_ref, loc, send1, recv1, send2, recv2, between):
    nrow, bands, passes, _ = sizes
    p = lax.axis_index("pass")
    b = lax.axis_index("tile") * nrow + lax.axis_index("row")
    own = pltpu.make_async_copy(packed.at[b], o_ref.at[p, b], loc)
    pending = []

    def forward(src, slot, index):
        for k in range(1, passes):
            copy = pltpu.make_async_remote_copy(
                src_ref=src,
                dst_ref=o_ref.at[p, index],
                send_sem=send2.at[k - 1, slot],
                recv_sem=recv2.at[k - 1, slot],
                device_id={"pass": (p + k) % passes},
                device_id_type=MESH,
            )
            copy.start()
            pending.append(copy)

    forward(packed.at[b], 0, b)
    first = []
    for k in range(1, bands):
        peer, _ = partners(b, k, bands)
        copy = pltpu.make_async_remote_copy(
            src_ref=packed.at[peer],
            dst_ref=o_ref.at[p, b],
            send_sem=send1.at[k - 1],
            recv_sem=recv1.at[k - 1],
            device_id={"tile": peer // nrow, "row": peer % nrow},
            device_id_type=MESH,
        )
        copy.start()
        first.append((k, copy))
    own.start()
    for k, copy in first:
        if between:
            between.pop(0)()
        copy.wait_recv()
        _, source = partners(b, k, bands)
        forward(o_ref.at[p, source], k, source)
    for step in between:
        step()
    for _, copy in first:
        copy.wait_send()
    for copy in pending:
        copy.wait()
    own.wait()


def first_kernel(sizes, cols, *refs):
    hbm, refs = refs[:14], refs[14:]
    o_ref, list_ref, which, t_qkv, t_out, t_in, t_w1, t_w2, t_gains = refs[:9]
    packed, mine, table, codes, plan, shifts, flags, x_ref, *vmem = refs[9:28]
    loads, move, send, recv, *sems = refs[28:]
    w_query, w_key, w_value, w_out, w_in, w1, w2 = vmem[:7]
    nrow, bands, passes, groups = sizes
    per, own_cols, _, _ = x_ref.shape
    slots, chans, rows = o_ref.shape[3:]
    ncols = own_cols * bands
    g = lax.axis_index("groups")
    p = lax.axis_index("pass")
    b = lax.axis_index("tile") * nrow + lax.axis_index("row")
    peers = [(dg, dp) for dg in range(groups) for dp in range(passes) if (dg, dp) != (0, 0)]
    copies = [
        pltpu.make_async_copy(source, target, loads.at[n])
        for n, (source, target) in enumerate(zip(hbm, [shifts, x_ref, flags, *vmem]))
    ]
    for copy in copies[:2]:
        copy.start()
    barrier, greeted = enter(True, sizes)
    for copy in copies[2:]:
        copy.start()
    copies[0].wait()

    offs = [shifts[1, r] for r in range(per)]
    picked = []
    for c in range(own_cols):
        for n, r in enumerate(chosen_of(b * own_cols + c, offs, ncols, list(range(slots)))):
            picked.append((c, n, r, shifts[0, r]))
    lanes = lax.broadcasted_iota(jnp.int32, (1, mine.shape[1]), 1)
    for r in range(per):
        col = lanes + offs[r]
        slot = jnp.zeros_like(lanes)
        for q in range(r):
            slot = slot + inside(col - offs[q], ncols).astype(jnp.int32)
        live = inside(col, ncols) & (lanes < ncols)
        mine[r : r + 1, :] = jnp.where(live, slot * ncols + col, -1)
    copies[1].wait()
    for c, n, r, offset in picked:
        roll_rows(x_ref, packed, c, n, r, offset)

    pl.semaphore_wait(barrier, greeted)
    metas = [pltpu.make_async_copy(mine, table.at[0, p], move.at[0])]
    metas[0].start()
    for n, (dg, dp) in enumerate(peers):
        copy = pltpu.make_async_remote_copy(
            src_ref=mine,
            dst_ref=table.at[(groups - dg) % groups, p],
            send_sem=send.at[n],
            recv_sem=recv.at[n],
            device_id={"groups": (g + dg) % groups, "pass": (p + dp) % passes},
            device_id_type=MESH,
        )
        copy.start()
        metas.append(copy)

    count = passes * per
    spots = lax.broadcasted_iota(jnp.int32, (1, list_ref.shape[1]), 1)
    moved = pltpu.make_async_copy(table.at[0], codes, move.at[1])
    told = pltpu.make_async_copy(plan, which, move.at[2])
    sizes_of = [jnp.zeros_like(spots)]

    def prepare():
        for copy in copies[2:]:
            copy.wait()
        for i, ref in enumerate((w_query, w_key, w_value)):
            t_qkv[i * chans : (i + 1) * chans, :] = ref[...].T
        t_out[...] = w_out[...].T
        t_in[...] = w_in[...].T
        t_w1[...] = w1[...].T
        for i, ref in enumerate(vmem[7:]):
            t_gains[i] = jnp.broadcast_to(ref[...], (rows, chans)).T
        for i in range(w2.shape[0]):
            taps = w2[i].astype(f32)
            for j in range(w2.shape[2]):
                at = (i * w2.shape[2] + j) * chans
                t_w2[:, at : at + chans] = taps[:, j, :].astype(half)

    def gathered():
        for copy in metas:
            copy.wait()
        moved.start()
        held = table[...]
        alive = [
            sum((held[i, j] >= 0).astype(jnp.int32).sum(axis=0) for j in range(passes))
            for i in range(groups)
        ]
        busiest = jnp.max(functools.reduce(jnp.maximum, alive))
        more = lax.div(jnp.max(held), ncols) + 1 - slots
        plain = sum((busiest > width).astype(jnp.int32) for width in widths(count)[:-1])
        if per > slots:
            late = len(widths(count)) + jnp.where(
                more > 1, 2, jnp.where(busiest > widths(count)[-3], 1, 0)
            )
            plain = jnp.where(more > 0, late, plain)
        plan[0] = plain
        told.start()

    def listed(x):
        def step():
            if x == 0:
                moved.wait()
            token = jnp.zeros_like(spots)
            at = jnp.int32(0)
            total = jnp.int32(0)
            for r in range(count):
                code = codes[r // per, r % per, p * cols + x]
                flag = flags[0, r]
                live = flag * (code >= 0).astype(jnp.int32)
                place = (r // per * ncols + lax.rem(code, ncols)) * per + lax.div(code, ncols)
                token = jnp.where(spots == at, (place + 1) * live, token)
                at = at + live
                total = total + flag
            list_ref[x : x + 1, :] = token
            sizes_of[0] = jnp.where(spots == x, at, sizes_of[0])
            if x == cols - 1:
                list_ref[cols : cols + 1, :] = jnp.zeros_like(spots)
                list_ref[cols + 1 : cols + 2, :] = jnp.where(spots == cols + 1, total, sizes_of[0])

        return step

    steps = [prepare, lambda: None, gathered] + [listed(x) for x in range(cols)]
    exchange(sizes, packed, o_ref, *sems, steps)
    told.wait()


def rest_kernel(sizes, skip, s_hbm, x_hbm, o_ref, packed, shifts, x_ref, loads, *sems):
    nrow, bands, _, _ = sizes
    per, own_cols, _, _ = x_ref.shape
    slots = o_ref.shape[3]
    ncols = own_cols * bands
    b = lax.axis_index("tile") * nrow + lax.axis_index("row")
    copies = [
        pltpu.make_async_copy(s_hbm, shifts, loads.at[0]),
        pltpu.make_async_copy(x_hbm, x_ref, loads.at[1]),
    ]
    for copy in copies:
        copy.start()
    barrier, greeted = enter(False, sizes)
    for copy in copies:
        copy.wait()
    offs = [shifts[1, r] for r in range(per)]
    wanted = list(range(skip, skip + slots))
    for c in range(own_cols):
        for n, r in enumerate(chosen_of(b * own_cols + c, offs, ncols, wanted)):
            roll_rows(x_ref, packed, c, n, r, shifts[0, r])
    pl.semaphore_wait(barrier, greeted)
    exchange(sizes, packed, o_ref, *sems, [])


def rms(values, gain):
    mean = jnp.mean(values * values, axis=0, keepdims=True)
    return values * lax.rsqrt(mean + eps) * gain


MOVES = [(dp, db) for dp in (-1, 1) for db in (-1, 1)] + [(0, -1), (0, 1), (-1, 0), (1, 0)]


def cut(total, most):
    batches = -(-total // most)
    return batches, -(-total // batches)


def finish_kernel(sizes, per, width, *refs):
    tokens_v, gains, w_qkv, w_out, w_in, w_back, w1, w2 = refs[:8]
    *pieces, o_ref, q_s, k_s, v_s, mixed_s, total_s, j_ref, edges = refs[8 : -len(MOVES) - 6]
    bufs = refs[-len(MOVES) - 6 : -6]
    taps, acts, tokens, load, send, recv = refs[-6:]
    listed = pltpu.make_async_copy(tokens_v, tokens, load)
    listed.start()
    nrow, bands, passes = sizes
    cols, chans, rows = j_ref.shape
    head = chans // HEADS
    scale = 1.0 / math.sqrt(head)
    held = [ref.shape[1] for ref in pieces]
    p = lax.axis_index("pass")
    b = lax.axis_index("tile") * nrow + lax.axis_index("row")

    def exists(dp, db):
        ok = jnp.bool_(True)
        if dp:
            ok = ok & (p + dp >= 0) & (p + dp < passes)
        if db:
            ok = ok & (b + db >= 0) & (b + db < bands)
        return ok

    def target(dp, db):
        k = b + db
        return {"pass": p + dp, "tile": k // nrow, "row": k % nrow}

    barrier = pltpu.get_barrier_semaphore()
    neighbours = jnp.int32(0)
    for dp, db in MOVES:
        there = exists(dp, db)
        neighbours = neighbours + there.astype(jnp.int32)

        @pl.when(there)
        def _():
            pl.semaphore_signal(barrier, inc=1, device_id=target(dp, db), device_id_type=MESH)

    listed.wait()
    flag_sum = tokens[cols + 1, cols + 1].astype(f32)

    def cell_of(x, j):
        code = tokens[x, j]
        place = jnp.maximum(code - 1, 0)
        source, slot = lax.div(place, per), lax.rem(place, per)
        cell = pieces[0][source, jnp.minimum(slot, held[0] - 1)].astype(f32)
        if len(pieces) > 1:
            later = pieces[1][source, jnp.clip(slot - held[0], 0, held[1] - 1)].astype(f32)
            cell = jnp.where(slot < held[0], cell, later)
        return jnp.where(code > 0, cell, 0.0)

    def part(values, i):
        return values[:, i * rows : (i + 1) * rows]

    batches, batch = cut(cols * width, PROJECT)

    def project(n, carry):
        g1, gq, gk = gains[0], gains[1], gains[2]
        places = [n * batch + i for i in range(batch)]
        normed = [
            rms(cell_of(lax.div(t, width), lax.rem(t, width)), g1).astype(half) for t in places
        ]
        qkv = dot(w_qkv[...], jnp.concatenate(normed, axis=1))
        for i, t in enumerate(places):
            one = part(qkv, i)
            q_s[t] = rms(one[:chans], gq * scale)
            k_s[t] = rms(one[chans : 2 * chans], gk)
            v_s[t] = one[2 * chans :]
        return carry

    lax.fori_loop(0, batches, project, 0)
    short = width <= 6

    def column(x, carry):
        size = tokens[cols + 1, x]
        dead = flag_sum - size.astype(f32)
        base = x * width

        def keys_of(queries, keys, sums):
            out = []
            for query, (above, below) in zip(queries, sums):
                q = q_s[base + query]
                for k in keys:
                    prod = (q * k_s[base + k]).reshape(HEADS, head, rows)
                    weight = jnp.exp(jnp.sum(prod, axis=1, keepdims=True))
                    weight = weight * jnp.where(k < size, 1.0, 0.0)
                    above = above + weight * v_s[base + k].reshape(HEADS, head, rows)
                    below = below + weight
                out.append((above, below))
            return tuple(out)

        def attend(queries):
            sums = tuple(
                (jnp.zeros((HEADS, head, rows), f32), jnp.full((HEADS, 1, rows), dead, f32))
                for _ in queries
            )
            if short:
                sums = keys_of(queries, range(width), sums)
            else:
                sums = lax.fori_loop(
                    0,
                    width // KEYS,
                    lambda n, sums: keys_of(queries, [n * KEYS + u for u in range(KEYS)], sums),
                    sums,
                )
            for query, (above, below) in zip(queries, sums):
                mixed = (above * (1.0 / below)).reshape(chans, rows)
                mixed_s[x * (width + 1) + query] = mixed.astype(half)

        if short:
            for query in range(0, width, QUERIES):
                attend(list(range(query, min(query + QUERIES, width))))
        else:

            def some(n, carry):
                attend([n * QUERIES + i for i in range(QUERIES)])
                return carry

            lax.fori_loop(0, width // QUERIES, some, 0)
        if short:
            shared = jnp.zeros((chans, rows), f32)
            for k in range(width):
                shared = shared + v_s[base + k]
        else:
            shared = lax.fori_loop(
                0, width, lambda k, total: total + v_s[base + k], jnp.zeros((chans, rows), f32)
            )
        mixed_s[x * (width + 1) + width] = (shared / flag_sum).astype(half)
        return carry

    lax.fori_loop(0, cols, column, 0)
    total_s[...] = jnp.zeros_like(total_s)
    steps, step = cut(cols * (width + 1), BATCH)

    def feed(n, carry):
        places = [n * step + i for i in range(step)]
        where = [(lax.div(t, width + 1), lax.rem(t, width + 1)) for t in places]
        back = dot(w_out[...], jnp.concatenate([mixed_s[t] for t in places], axis=1))
        g2 = gains[3]
        hidden = [cell_of(*at) + part(back, i) for i, at in enumerate(where)]
        normed = [rms(one, g2).astype(half) for one in hidden]
        inner = gelu(dot(w_in[...], jnp.concatenate(normed, axis=1)))
        added = dot(w_back[...], inner.astype(half))
        for i, (x, j) in enumerate(where):
            size = tokens[cols + 1, x]
            dead = flag_sum - size.astype(f32)
            weight = jnp.where(j < size, 1.0, jnp.where(j == width, dead, 0.0))
            total_s[x] += (hidden[i] + part(added, i)) * weight
        return carry

    lax.fori_loop(0, steps, feed, 0)
    folds = chans // TILE
    strip = rows // (cols * folds)
    fold_lane = lax.broadcasted_iota(jnp.int32, (TILE, rows), 1)
    top = bottom = jnp.zeros((TILE, rows), f32)
    for x in range(cols):
        joined = total_s[x] / flag_sum
        j_ref[x] = joined.astype(half)
        for f in range(folds):
            piece = joined[f * TILE : (f + 1) * TILE]
            at = (f * cols + x) * strip
            here = (fold_lane >= at) & (fold_lane < at + strip)
            top = jnp.where(here, pltpu.roll(piece, at, 1), top)
            bottom = jnp.where(here, pltpu.roll(piece, (at + strip) % rows, 1), bottom)
    edges[0] = top.astype(half)
    edges[1] = bottom.astype(half)

    pl.semaphore_wait(barrier, neighbours)

    def copy_of(n):
        dp, db = MOVES[n]
        if db:
            src = edges.at[0 if db < 0 else 1]
        else:
            src = j_ref.at[pl.ds(cols - 2 if dp > 0 else 0, 2)]
        return pltpu.make_async_remote_copy(
            src_ref=src,
            dst_ref=bufs[n],
            send_sem=send.at[n],
            recv_sem=recv.at[n],
            device_id=target(dp, db),
            device_id_type=MESH,
        )

    for n, (dp, db) in enumerate(MOVES):

        @pl.when(exists(dp, db))
        def _():
            copy_of(n).start()

    for n, (dp, db) in enumerate(MOVES):

        @pl.when(exists(-dp, -db))
        def _():
            copy_of(n).wait_recv()

        @pl.when(jnp.logical_not(exists(-dp, -db)))
        def _():
            bufs[n][...] = jnp.zeros_like(bufs[n])

    def side(dp, db):
        return bufs[MOVES.index((-dp, -db))]

    lane = lax.broadcasted_iota(jnp.int32, (chans, rows), 1)
    wide_lane = lax.broadcasted_iota(jnp.int32, (chans, 2 * rows), 1)

    def widen(values):
        last = 2 * rows - 1
        return jnp.concatenate(
            [
                pltpu.roll(values, 1, 1).astype(half),
                values.astype(half),
                pltpu.roll(values, last, 1).astype(half),
            ],
            axis=0,
        )

    for n in range(cols + 4):
        dp = -1 if n < 2 else (1 if n >= cols + 2 else 0)
        at = n if dp < 0 else (n - cols - 2 if dp > 0 else n - 2)
        middle = j_ref[at] if dp == 0 else side(dp, 0)[at]
        col = cols - 2 + n if dp < 0 else at
        above, below = side(dp, -1)[...].astype(f32), side(dp, 1)[...].astype(f32)
        spots = [(f * cols + col) * strip for f in range(folds)]
        after = jnp.concatenate([pltpu.roll(below, (rows - s) % rows, 1) for s in spots], axis=0)
        before = jnp.concatenate([pltpu.roll(above, rows - strip - s, 1) for s in spots], axis=0)
        border = jnp.where(lane < rows // 2, after, before)
        taps[n] = widen(jnp.concatenate([middle.astype(f32), border], axis=1))
    row_pos = b * rows + jnp.where(wide_lane < rows + rows // 2, wide_lane, wide_lane - 2 * rows)
    row_inside = (row_pos >= 0) & (row_pos < bands * rows)
    for n in range(cols + 2):
        near = taps[n : n + 3].reshape(9 * chans, 2 * rows)
        act = gelu(dot(w1[...], near))
        col_pos = p * cols + n - 1
        inside = row_inside & (col_pos >= 0) & (col_pos < passes * cols)
        acts[n] = widen(jnp.where(inside, act, 0.0))
    near = [acts[n : n + 3, :, :rows].reshape(9 * chans, rows) for n in range(cols)]
    result = dot(w2[...], jnp.concatenate(near, axis=1))
    for n in range(cols):
        o_ref[n] = part(result, n)

    for n, (dp, db) in enumerate(MOVES):

        @pl.when(exists(dp, db))
        def _():
            copy_of(n).wait_send()


def local(
    sizes,
    revisits,
    shifts,
    flags,
    norm1_gain,
    w_query,
    w_key,
    w_value,
    query_gain,
    key_gain,
    w_out,
    norm2_gain,
    w_in,
    w_back,
    conv_first,
    conv_second,
):
    nrow, bands, passes, groups = sizes
    per, own_cols, chans, all_rows = revisits.shape
    rows = all_rows // bands
    ncols = own_cols * bands
    cols = ncols // passes
    count = per * passes
    outs = conv_second.shape[3]
    hidden = w_in.shape[1]
    dma = pltpu.SemaphoreType.DMA
    peers = max(groups * passes - 1, 1)
    shape = jax.ShapeDtypeStruct
    slots = min(SLOTS, per)
    others = max(passes - 1, 1)
    exchange_sems = [dma, dma((bands,)), dma((bands,)), dma((others, bands)), dma((others, bands))]

    def in_hbm(*arrays):
        return [pltpu.with_memory_space_constraint(array, pltpu.HBM) for array in arrays]

    operands = (
        shifts.T,
        revisits,
        flags.T,
        w_query,
        w_key,
        w_value,
        w_out,
        w_in,
        conv_first.reshape(9 * chans, -1),
        conv_second.transpose(0, 3, 1, 2),
        *(gain.reshape(1, chans) for gain in (norm1_gain, query_gain, key_gain, norm2_gain)),
    )
    results = (
        shape((passes, bands, own_cols, slots, chans, rows), half),
        shape(((cols + 2 + 7) // 8 * 8, 128), jnp.int32),
        shape((1,), jnp.int32),
        shape((3 * chans, chans), half),
        shape((chans, chans), half),
        shape((hidden, chans), half),
        shape((chans, 9 * chans), half),
        shape((outs, 9 * chans), half),
        shape((4, chans, rows), f32),
    )
    banded, tokens, which, t_qkv, t_out, t_in, t_w1, t_w2, gains = pl.pallas_call(
        functools.partial(first_kernel, sizes, cols),
        out_shape=results,
        in_specs=[whole(pltpu.HBM)] * len(operands),
        out_specs=tuple(whole(pltpu.HBM) if n == 2 else whole() for n in range(len(results))),
        scratch_shapes=[
            pltpu.VMEM((bands, own_cols, slots, chans, rows), half),
            pltpu.VMEM((per, 128), jnp.int32),
            pltpu.VMEM((groups, passes, per, 128), jnp.int32),
            pltpu.SMEM((passes, per, 128), jnp.int32),
            pltpu.SMEM((1,), jnp.int32),
            pltpu.SMEM((2, per), jnp.int32),
            pltpu.SMEM((1, count), jnp.int32),
            pltpu.VMEM(revisits.shape, half),
            *(pltpu.VMEM(array.shape, array.dtype) for array in operands[3:]),
            dma((len(operands),)),
            dma((3,)),
            dma((peers,)),
            dma((peers,)),
            *exchange_sems,
        ],
        compiler_params=pltpu.CompilerParams(
            collective_id=0, has_side_effects=True, vmem_limit_bytes=16 * MIB
        ),
        name="first",
    )(*in_hbm(*operands))

    def finish(width, identity, tokens, weights, *pieces):
        batches, batch = cut(cols * width, PROJECT)
        steps, step = cut(cols * (width + 1), BATCH)
        return pl.pallas_call(
            functools.partial(finish_kernel, sizes[:3], per, width),
            out_shape=shape((cols, outs, rows), f32),
            in_specs=[whole()] * (1 + len(weights) + len(pieces)),
            out_specs=whole(),
            scratch_shapes=[
                pltpu.VMEM((batches * batch, chans, rows), f32),
                pltpu.VMEM((batches * batch, chans, rows), f32),
                pltpu.VMEM((batches * batch, chans, rows), f32),
                pltpu.VMEM((steps * step, chans, rows), half),
                pltpu.VMEM((cols + 1, chans, rows), f32),
                pltpu.VMEM((cols, chans, rows), half),
                pltpu.VMEM((2, TILE, rows), half),
                *(
                    pltpu.VMEM((TILE, rows) if db else (2, chans, rows), half)
                    for dp, db in MOVES
                ),
                pltpu.VMEM((cols + 4, 3 * chans, 2 * rows), half),
                pltpu.VMEM((cols + 2, 3 * chans, 2 * rows), half),
                pltpu.SMEM(tokens.shape, jnp.int32),
                dma,
                dma((len(MOVES),)),
                dma((len(MOVES),)),
            ],
            compiler_params=pltpu.CompilerParams(
                collective_id=identity, has_side_effects=True, vmem_limit_bytes=24 * MIB
            ),
            name="finish",
        )(tokens, *weights, *(ref.reshape(passes * ncols, -1, chans, rows) for ref in pieces))

    def branch(n, more, width):
        def run(tokens, weights, banded, shifts, revisits):
            if not more:
                return finish(width, 1 + 2 * n, tokens, weights, banded)
            rest = pl.pallas_call(
                functools.partial(rest_kernel, sizes, slots),
                out_shape=shape((passes, bands, own_cols, more, chans, rows), half),
                in_specs=[whole(pltpu.HBM)] * 2,
                out_specs=whole(),
                scratch_shapes=[
                    pltpu.VMEM((bands, own_cols, more, chans, rows), half),
                    pltpu.SMEM((2, per), jnp.int32),
                    pltpu.VMEM(revisits.shape, half),
                    dma((2,)),
                    *exchange_sems,
                ],
                compiler_params=pltpu.CompilerParams(
                    collective_id=2 + 2 * n, has_side_effects=True, vmem_limit_bytes=16 * MIB
                ),
                name="rest",
            )(*in_hbm(shifts, revisits))
            return finish(width, 1 + 2 * n, tokens, weights, banded, rest)

        return run

    weights = (gains, t_qkv, t_out, t_in, w_back.T, t_w1, t_w2)
    plans = [(0, width) for width in widths(count)]
    if per > slots:
        plans += [(1, widths(count)[-3]), (1, count), (per - slots, count)]
    branches = [branch(n, *plan) for n, plan in enumerate(plans)]
    return lax.switch(which[0], branches, tokens, weights, banded, shifts.T, revisits)


def solution(mesh):
    shape = mesh.shape
    sizes = (shape["row"], shape["tile"] * shape["row"], shape["pass"], shape["groups"])
    fixed = [P()] * 12
    return jax.shard_map(
        functools.partial(local, sizes),
        mesh=mesh,
        in_specs=(
            P(("groups", "pass"), ("tile", "row"), None, None),
            P(("groups", "pass"), None),
            P("groups", ("tile", "row")),
            *fixed,
        ),
        out_specs=P(("groups", "pass"), None, ("tile", "row")),
        check_vma=False,
    )
```

```python
import functools
import math

import jax
import jax.numpy as jnp
import numpy as np
from jax import lax
from jax.experimental import pallas as pl
from jax.experimental.pallas import tpu as pltpu
from jax.sharding import PartitionSpec as P

HEADS = 4
eps = 1e-05
f32 = jnp.float32
half = jnp.bfloat16
MESH = pl.DeviceIdType.MESH
MIB = 1024 * 1024
PROJECT = 8
BATCH = 10
QUERIES = 2
KEYS = 4
SLOTS = 3
TILE = 16


def whole(space=pltpu.VMEM):
    return pl.BlockSpec(memory_space=space)


def dot(weights, values):
    return jnp.dot(weights, values, preferred_element_type=f32)


GELU = math.sqrt(2.0 / math.pi)


def gelu(x):
    shaped = x * (GELU + (GELU * 0.044715) * (x * x))
    halved = 0.5 * x
    return halved + halved * jnp.tanh(shaped)


def inside(col, ncols):
    return (col >= 0) & (col < ncols)


def partners(b, k, bands):
    if bands & (bands - 1):
        return lax.rem(b + k, bands), lax.rem(b + bands - k, bands)
    out, bit = 0, 1
    while bit < bands:
        own = lax.rem(lax.div(b, bit), 2)
        out = out + bit * (1 - own if k // bit % 2 else own)
        bit *= 2
    return out, out


def widths(count):
    return [width for width in (2, 3, 4, 5, 6, 8) if width < count] + [count]


def enter(groups_too, sizes):
    nrow, bands, passes, groups = sizes
    g = lax.axis_index("groups")
    p = lax.axis_index("pass")
    b = lax.axis_index("tile") * nrow + lax.axis_index("row")
    barrier = pltpu.get_barrier_semaphore()
    targets = []
    for k in range(1, bands):
        peer = lax.rem(b + k, bands)
        targets.append({"tile": peer // nrow, "row": peer % nrow})
    for dg in range(groups if groups_too else 1):
        for dp in range(passes):
            if (dg, dp) != (0, 0):
                targets.append({"groups": (g + dg) % groups, "pass": (p + dp) % passes})
    for target in targets:
        pl.semaphore_signal(barrier, inc=1, device_id=target, device_id_type=MESH)
    return barrier, len(targets)


def chosen_of(col, cols, ncols, wanted):
    rank = jnp.int32(0)
    chosen = [jnp.int32(0)] * len(wanted)
    for r, offset in enumerate(cols):
        live = inside(col - offset, ncols).astype(jnp.int32)
        for n, k in enumerate(wanted):
            if k <= r:
                chosen[n] = chosen[n] + r * live * (rank == k).astype(jnp.int32)
        rank = rank + live
    return chosen


def roll_rows(x_ref, packed, c, n, r, offset):
    bands, _, _, chans, rows = packed.shape
    lane = lax.broadcasted_iota(jnp.int32, (chans, rows), 1)
    zero = jnp.zeros((chans, rows), f32)
    amount = lax.rem(2 * rows - offset, rows)
    pos = lane + offset
    rolled = [
        pltpu.roll(x_ref[r, c, :, t * rows : (t + 1) * rows].astype(f32), amount, 1)
        for t in range(bands)
    ]
    for t in range(bands):
        low = rolled[t - 1] if t else zero
        high = rolled[t + 1] if t + 1 < bands else zero
        out = jnp.where(pos < 0, low, jnp.where(pos >= rows, high, rolled[t]))
        packed[t, c, n] = out.astype(half)


def exchange(sizes, packed, o_ref, loc, send1, recv1, send2, recv2, between):
    nrow, bands, passes, _ = sizes
    p = lax.axis_index("pass")
    b = lax.axis_index("tile") * nrow + lax.axis_index("row")
    own = pltpu.make_async_copy(packed.at[b], o_ref.at[p, b], loc)
    pending = []

    def forward(src, slot, index):
        for k in range(1, passes):
            copy = pltpu.make_async_remote_copy(
                src_ref=src,
                dst_ref=o_ref.at[p, index],
                send_sem=send2.at[k - 1, slot],
                recv_sem=recv2.at[k - 1, slot],
                device_id={"pass": (p + k) % passes},
                device_id_type=MESH,
            )
            copy.start()
            pending.append(copy)

    forward(packed.at[b], 0, b)
    first = []
    for k in range(1, bands):
        peer, _ = partners(b, k, bands)
        copy = pltpu.make_async_remote_copy(
            src_ref=packed.at[peer],
            dst_ref=o_ref.at[p, b],
            send_sem=send1.at[k - 1],
            recv_sem=recv1.at[k - 1],
            device_id={"tile": peer // nrow, "row": peer % nrow},
            device_id_type=MESH,
        )
        copy.start()
        first.append((k, copy))
    own.start()
    for k, copy in first:
        if between:
            between.pop(0)()
        copy.wait_recv()
        _, source = partners(b, k, bands)
        forward(o_ref.at[p, source], k, source)
    for step in between:
        step()
    for _, copy in first:
        copy.wait_send()
    for copy in pending:
        copy.wait()
    own.wait()


def first_kernel(sizes, cols, *refs):
    hbm, refs = refs[:14], refs[14:]
    o_ref, list_ref, which, t_qkv, t_out, t_in, t_w1, t_w2, t_gains = refs[:9]
    packed, mine, table, codes, plan, shifts, flags, x_ref, *vmem = refs[9:28]
    loads, move, send, recv, *sems = refs[28:]
    w_query, w_key, w_value, w_out, w_in, w1, w2 = vmem[:7]
    nrow, bands, passes, groups = sizes
    per, own_cols, _, _ = x_ref.shape
    slots, chans, rows = o_ref.shape[3:]
    ncols = own_cols * bands
    g = lax.axis_index("groups")
    p = lax.axis_index("pass")
    b = lax.axis_index("tile") * nrow + lax.axis_index("row")
    peers = [(dg, dp) for dg in range(groups) for dp in range(passes) if (dg, dp) != (0, 0)]
    copies = [
        pltpu.make_async_copy(source, target, loads.at[n])
        for n, (source, target) in enumerate(zip(hbm, [shifts, x_ref, flags, *vmem]))
    ]
    for copy in copies[:2]:
        copy.start()
    barrier, greeted = enter(True, sizes)
    for copy in copies[2:]:
        copy.start()
    copies[0].wait()

    offs = [shifts[1, r] for r in range(per)]
    picked = []
    for c in range(own_cols):
        for n, r in enumerate(chosen_of(b * own_cols + c, offs, ncols, list(range(slots)))):
            picked.append((c, n, r, shifts[0, r]))
    lanes = lax.broadcasted_iota(jnp.int32, (1, mine.shape[1]), 1)
    for r in range(per):
        col = lanes + offs[r]
        slot = jnp.zeros_like(lanes)
        for q in range(r):
            slot = slot + inside(col - offs[q], ncols).astype(jnp.int32)
        live = inside(col, ncols) & (lanes < ncols)
        mine[r : r + 1, :] = jnp.where(live, slot * ncols + col, -1)
    copies[1].wait()
    for c, n, r, offset in picked:
        roll_rows(x_ref, packed, c, n, r, offset)

    pl.semaphore_wait(barrier, greeted)
    metas = [pltpu.make_async_copy(mine, table.at[0, p], move.at[0])]
    metas[0].start()
    for n, (dg, dp) in enumerate(peers):
        copy = pltpu.make_async_remote_copy(
            src_ref=mine,
            dst_ref=table.at[(groups - dg) % groups, p],
            send_sem=send.at[n],
            recv_sem=recv.at[n],
            device_id={"groups": (g + dg) % groups, "pass": (p + dp) % passes},
            device_id_type=MESH,
        )
        copy.start()
        metas.append(copy)

    count = passes * per
    spots = lax.broadcasted_iota(jnp.int32, (1, list_ref.shape[1]), 1)
    moved = pltpu.make_async_copy(table.at[0], codes, move.at[1])
    told = pltpu.make_async_copy(plan, which, move.at[2])
    sizes_of = [jnp.zeros_like(spots)]

    def prepare():
        for copy in copies[2:]:
            copy.wait()
        for i, ref in enumerate((w_query, w_key, w_value)):
            t_qkv[i * chans : (i + 1) * chans, :] = ref[...].T
        t_out[...] = w_out[...].T
        t_in[...] = w_in[...].T
        t_w1[...] = w1[...].T
        for i, ref in enumerate(vmem[7:]):
            t_gains[i] = jnp.broadcast_to(ref[...], (rows, chans)).T
        for i in range(w2.shape[0]):
            taps = w2[i].astype(f32)
            for j in range(w2.shape[2]):
                at = (i * w2.shape[2] + j) * chans
                t_w2[:, at : at + chans] = taps[:, j, :].astype(half)

    def gathered():
        for copy in metas:
            copy.wait()
        moved.start()
        held = table[...]
        alive = [
            sum((held[i, j] >= 0).astype(jnp.int32).sum(axis=0) for j in range(passes))
            for i in range(groups)
        ]
        busiest = jnp.max(functools.reduce(jnp.maximum, alive))
        more = lax.div(jnp.max(held), ncols) + 1 - slots
        plain = sum((busiest > width).astype(jnp.int32) for width in widths(count)[:-1])
        if per > slots:
            late = len(widths(count)) + jnp.where(
                more > 1, 2, jnp.where(busiest > widths(count)[-3], 1, 0)
            )
            plain = jnp.where(more > 0, late, plain)
        plan[0] = plain
        told.start()

    def listed(x):
        def step():
            if x == 0:
                moved.wait()
            token = jnp.zeros_like(spots)
            at = jnp.int32(0)
            total = jnp.int32(0)
            for r in range(count):
                code = codes[r // per, r % per, p * cols + x]
                flag = flags[0, r]
                live = flag * (code >= 0).astype(jnp.int32)
                place = (r // per * ncols + lax.rem(code, ncols)) * per + lax.div(code, ncols)
                token = jnp.where(spots == at, (place + 1) * live, token)
                at = at + live
                total = total + flag
            list_ref[x : x + 1, :] = token
            sizes_of[0] = jnp.where(spots == x, at, sizes_of[0])
            if x == cols - 1:
                list_ref[cols : cols + 1, :] = jnp.zeros_like(spots)
                list_ref[cols + 1 : cols + 2, :] = jnp.where(spots == cols + 1, total, sizes_of[0])

        return step

    steps = [prepare, lambda: None, gathered] + [listed(x) for x in range(cols)]
    exchange(sizes, packed, o_ref, *sems, steps)
    told.wait()


def rest_kernel(sizes, skip, s_hbm, x_hbm, o_ref, packed, shifts, x_ref, loads, *sems):
    nrow, bands, _, _ = sizes
    per, own_cols, _, _ = x_ref.shape
    slots = o_ref.shape[3]
    ncols = own_cols * bands
    b = lax.axis_index("tile") * nrow + lax.axis_index("row")
    copies = [
        pltpu.make_async_copy(s_hbm, shifts, loads.at[0]),
        pltpu.make_async_copy(x_hbm, x_ref, loads.at[1]),
    ]
    for copy in copies:
        copy.start()
    barrier, greeted = enter(False, sizes)
    for copy in copies:
        copy.wait()
    offs = [shifts[1, r] for r in range(per)]
    wanted = list(range(skip, skip + slots))
    for c in range(own_cols):
        for n, r in enumerate(chosen_of(b * own_cols + c, offs, ncols, wanted)):
            roll_rows(x_ref, packed, c, n, r, shifts[0, r])
    pl.semaphore_wait(barrier, greeted)
    exchange(sizes, packed, o_ref, *sems, [])


def rms(values, gain):
    mean = jnp.mean(values * values, axis=0, keepdims=True)
    return values * lax.rsqrt(mean + eps) * gain


MOVES = [(-1, 0), (1, 0), (0, -1), (0, 1)] + [(dp, db) for dp in (-1, 1) for db in (-1, 1)]


def cut(total, most):
    batches = -(-total // most)
    return batches, -(-total // batches)


def finish_kernel(sizes, per, width, *refs):
    tokens_v, gains, w_qkv, w_out, w_in, w_back, w1, w2 = refs[:8]
    *pieces, o_ref, q_s, k_s, v_s, mixed_s, total_s, j_ref, edges = refs[8 : -len(MOVES) - 6]
    bufs = refs[-len(MOVES) - 6 : -6]
    taps, acts, tokens, load, send, recv = refs[-6:]
    listed = pltpu.make_async_copy(tokens_v, tokens, load)
    listed.start()
    nrow, bands, passes = sizes
    cols, chans, rows = j_ref.shape
    head = chans // HEADS
    scale = 1.0 / math.sqrt(head)
    held = [ref.shape[1] for ref in pieces]
    p = lax.axis_index("pass")
    b = lax.axis_index("tile") * nrow + lax.axis_index("row")

    def exists(dp, db):
        ok = jnp.bool_(True)
        if dp:
            ok = ok & (p + dp >= 0) & (p + dp < passes)
        if db:
            ok = ok & (b + db >= 0) & (b + db < bands)
        return ok

    def target(dp, db):
        k = b + db
        return {"pass": p + dp, "tile": k // nrow, "row": k % nrow}

    barrier = pltpu.get_barrier_semaphore()
    neighbours = jnp.int32(0)
    for dp, db in MOVES:
        there = exists(dp, db)
        neighbours = neighbours + there.astype(jnp.int32)

        @pl.when(there)
        def _():
            pl.semaphore_signal(barrier, inc=1, device_id=target(dp, db), device_id_type=MESH)

    listed.wait()
    flag_sum = tokens[cols + 1, cols + 1].astype(f32)

    def cell_of(x, j):
        code = tokens[x, j]
        place = jnp.maximum(code - 1, 0)
        source, slot = lax.div(place, per), lax.rem(place, per)
        cell = pieces[0][source, jnp.minimum(slot, held[0] - 1)].astype(f32)
        if len(pieces) > 1:
            later = pieces[1][source, jnp.clip(slot - held[0], 0, held[1] - 1)].astype(f32)
            cell = jnp.where(slot < held[0], cell, later)
        return jnp.where(code > 0, cell, 0.0)

    def part(values, i):
        return values[:, i * rows : (i + 1) * rows]

    batches, batch = cut(cols * width, PROJECT)

    def project(n, carry):
        g1, gq, gk = gains[0], gains[1], gains[2]
        places = [n * batch + i for i in range(batch)]
        normed = [
            rms(cell_of(lax.div(t, width), lax.rem(t, width)), g1).astype(half) for t in places
        ]
        qkv = dot(w_qkv[...], jnp.concatenate(normed, axis=1))
        for i, t in enumerate(places):
            one = part(qkv, i)
            q_s[t] = rms(one[:chans], gq * scale)
            k_s[t] = rms(one[chans : 2 * chans], gk)
            v_s[t] = one[2 * chans :]
        return carry

    lax.fori_loop(0, batches, project, 0)
    short = width <= 6

    def column(x, carry):
        size = tokens[cols + 1, x]
        dead = flag_sum - size.astype(f32)
        base = x * width

        def keys_of(queries, keys, sums):
            out = []
            for query, (above, below) in zip(queries, sums):
                q = q_s[base + query]
                for k in keys:
                    prod = (q * k_s[base + k]).reshape(HEADS, head, rows)
                    weight = jnp.exp(jnp.sum(prod, axis=1, keepdims=True))
                    weight = weight * jnp.where(k < size, 1.0, 0.0)
                    above = above + weight * v_s[base + k].reshape(HEADS, head, rows)
                    below = below + weight
                out.append((above, below))
            return tuple(out)

        def attend(queries):
            sums = tuple(
                (jnp.zeros((HEADS, head, rows), f32), jnp.full((HEADS, 1, rows), dead, f32))
                for _ in queries
            )
            if short:
                sums = keys_of(queries, range(width), sums)
            else:
                sums = lax.fori_loop(
                    0,
                    width // KEYS,
                    lambda n, sums: keys_of(queries, [n * KEYS + u for u in range(KEYS)], sums),
                    sums,
                )
            for query, (above, below) in zip(queries, sums):
                mixed = (above * (1.0 / below)).reshape(chans, rows)
                mixed_s[x * (width + 1) + query] = mixed.astype(half)

        if short:
            for query in range(0, width, QUERIES):
                attend(list(range(query, min(query + QUERIES, width))))
        else:

            def some(n, carry):
                attend([n * QUERIES + i for i in range(QUERIES)])
                return carry

            lax.fori_loop(0, width // QUERIES, some, 0)
        if short:
            shared = jnp.zeros((chans, rows), f32)
            for k in range(width):
                shared = shared + v_s[base + k]
        else:
            shared = lax.fori_loop(
                0, width, lambda k, total: total + v_s[base + k], jnp.zeros((chans, rows), f32)
            )
        mixed_s[x * (width + 1) + width] = (shared / flag_sum).astype(half)
        return carry

    lax.fori_loop(0, cols, column, 0)
    total_s[...] = jnp.zeros_like(total_s)
    steps, step = cut(cols * (width + 1), BATCH)

    def feed(n, carry):
        places = [n * step + i for i in range(step)]
        where = [(lax.div(t, width + 1), lax.rem(t, width + 1)) for t in places]
        back = dot(w_out[...], jnp.concatenate([mixed_s[t] for t in places], axis=1))
        g2 = gains[3]
        hidden = [cell_of(*at) + part(back, i) for i, at in enumerate(where)]
        normed = [rms(one, g2).astype(half) for one in hidden]
        inner = gelu(dot(w_in[...], jnp.concatenate(normed, axis=1)))
        added = dot(w_back[...], inner.astype(half))
        for i, (x, j) in enumerate(where):
            size = tokens[cols + 1, x]
            dead = flag_sum - size.astype(f32)
            weight = jnp.where(j < size, 1.0, jnp.where(j == width, dead, 0.0))
            total_s[x] += (hidden[i] + part(added, i)) * weight
        return carry

    lax.fori_loop(0, steps, feed, 0)
    folds = chans // TILE
    strip = rows // (cols * folds)
    fold_lane = lax.broadcasted_iota(jnp.int32, (TILE, rows), 1)
    top = bottom = jnp.zeros((TILE, rows), f32)
    for x in range(cols):
        joined = total_s[x] / flag_sum
        j_ref[x] = joined.astype(half)
        for f in range(folds):
            piece = joined[f * TILE : (f + 1) * TILE]
            at = (f * cols + x) * strip
            here = (fold_lane >= at) & (fold_lane < at + strip)
            top = jnp.where(here, pltpu.roll(piece, at, 1), top)
            bottom = jnp.where(here, pltpu.roll(piece, (at + strip) % rows, 1), bottom)
    edges[0] = top.astype(half)
    edges[1] = bottom.astype(half)

    pl.semaphore_wait(barrier, neighbours)

    def copy_of(n):
        dp, db = MOVES[n]
        if db:
            src = edges.at[0 if db < 0 else 1]
        else:
            src = j_ref.at[pl.ds(cols - 2 if dp > 0 else 0, 2)]
        return pltpu.make_async_remote_copy(
            src_ref=src,
            dst_ref=bufs[n],
            send_sem=send.at[n],
            recv_sem=recv.at[n],
            device_id=target(dp, db),
            device_id_type=MESH,
        )

    for n, (dp, db) in enumerate(MOVES):

        @pl.when(exists(dp, db))
        def _():
            copy_of(n).start()

    for n, (dp, db) in enumerate(MOVES):

        @pl.when(exists(-dp, -db))
        def _():
            copy_of(n).wait_recv()

        @pl.when(jnp.logical_not(exists(-dp, -db)))
        def _():
            bufs[n][...] = jnp.zeros_like(bufs[n])

    def side(dp, db):
        return bufs[MOVES.index((-dp, -db))]

    lane = lax.broadcasted_iota(jnp.int32, (chans, rows), 1)
    wide_lane = lax.broadcasted_iota(jnp.int32, (chans, 2 * rows), 1)

    def widen(values):
        last = 2 * rows - 1
        return jnp.concatenate(
            [
                pltpu.roll(values, 1, 1).astype(half),
                values.astype(half),
                pltpu.roll(values, last, 1).astype(half),
            ],
            axis=0,
        )

    for n in range(cols + 4):
        dp = -1 if n < 2 else (1 if n >= cols + 2 else 0)
        at = n if dp < 0 else (n - cols - 2 if dp > 0 else n - 2)
        middle = j_ref[at] if dp == 0 else side(dp, 0)[at]
        col = cols - 2 + n if dp < 0 else at
        above, below = side(dp, -1)[...].astype(f32), side(dp, 1)[...].astype(f32)
        spots = [(f * cols + col) * strip for f in range(folds)]
        after = jnp.concatenate([pltpu.roll(below, (rows - s) % rows, 1) for s in spots], axis=0)
        before = jnp.concatenate([pltpu.roll(above, rows - strip - s, 1) for s in spots], axis=0)
        border = jnp.where(lane < rows // 2, after, before)
        taps[n] = widen(jnp.concatenate([middle.astype(f32), border], axis=1))
    row_pos = b * rows + jnp.where(wide_lane < rows + rows // 2, wide_lane, wide_lane - 2 * rows)
    row_inside = (row_pos >= 0) & (row_pos < bands * rows)
    for n in range(cols + 2):
        near = taps[n : n + 3].reshape(9 * chans, 2 * rows)
        act = gelu(dot(w1[...], near))
        col_pos = p * cols + n - 1
        inside = row_inside & (col_pos >= 0) & (col_pos < passes * cols)
        acts[n] = widen(jnp.where(inside, act, 0.0))
    near = [acts[n : n + 3, :, :rows].reshape(9 * chans, rows) for n in range(cols)]
    result = dot(w2[...], jnp.concatenate(near, axis=1))
    for n in range(cols):
        o_ref[:, n, :] = part(result, n)

    for n, (dp, db) in enumerate(MOVES):

        @pl.when(exists(dp, db))
        def _():
            copy_of(n).wait_send()


def local(
    sizes,
    revisits,
    shifts,
    flags,
    norm1_gain,
    w_query,
    w_key,
    w_value,
    query_gain,
    key_gain,
    w_out,
    norm2_gain,
    w_in,
    w_back,
    conv_first,
    conv_second,
):
    nrow, bands, passes, groups = sizes
    per, own_cols, chans, all_rows = revisits.shape
    rows = all_rows // bands
    ncols = own_cols * bands
    cols = ncols // passes
    count = per * passes
    outs = conv_second.shape[3]
    hidden = w_in.shape[1]
    dma = pltpu.SemaphoreType.DMA
    peers = max(groups * passes - 1, 1)
    shape = jax.ShapeDtypeStruct
    slots = min(SLOTS, per)
    others = max(passes - 1, 1)
    exchange_sems = [dma, dma((bands,)), dma((bands,)), dma((others, bands)), dma((others, bands))]

    def in_hbm(*arrays):
        return [pltpu.with_memory_space_constraint(array, pltpu.HBM) for array in arrays]

    operands = (
        shifts.T,
        revisits,
        flags.T,
        w_query,
        w_key,
        w_value,
        w_out,
        w_in,
        conv_first.reshape(9 * chans, -1),
        conv_second.transpose(0, 3, 1, 2),
        *(gain.reshape(1, chans) for gain in (norm1_gain, query_gain, key_gain, norm2_gain)),
    )
    results = (
        shape((passes, bands, own_cols, slots, chans, rows), half),
        shape(((cols + 2 + 7) // 8 * 8, 128), jnp.int32),
        shape((1,), jnp.int32),
        shape((3 * chans, chans), half),
        shape((chans, chans), half),
        shape((hidden, chans), half),
        shape((chans, 9 * chans), half),
        shape((outs, 9 * chans), half),
        shape((4, chans, rows), f32),
    )
    banded, tokens, which, t_qkv, t_out, t_in, t_w1, t_w2, gains = pl.pallas_call(
        functools.partial(first_kernel, sizes, cols),
        out_shape=results,
        in_specs=[whole(pltpu.HBM)] * len(operands),
        out_specs=tuple(whole(pltpu.HBM) if n == 2 else whole() for n in range(len(results))),
        scratch_shapes=[
            pltpu.VMEM((bands, own_cols, slots, chans, rows), half),
            pltpu.VMEM((per, 128), jnp.int32),
            pltpu.VMEM((groups, passes, per, 128), jnp.int32),
            pltpu.SMEM((passes, per, 128), jnp.int32),
            pltpu.SMEM((1,), jnp.int32),
            pltpu.SMEM((2, per), jnp.int32),
            pltpu.SMEM((1, count), jnp.int32),
            pltpu.VMEM(revisits.shape, half),
            *(pltpu.VMEM(array.shape, array.dtype) for array in operands[3:]),
            dma((len(operands),)),
            dma((3,)),
            dma((peers,)),
            dma((peers,)),
            *exchange_sems,
        ],
        compiler_params=pltpu.CompilerParams(
            collective_id=0, has_side_effects=True, vmem_limit_bytes=16 * MIB
        ),
        name="first",
    )(*in_hbm(*operands))

    def finish(width, identity, tokens, weights, *pieces):
        batches, batch = cut(cols * width, PROJECT)
        steps, step = cut(cols * (width + 1), BATCH)
        return pl.pallas_call(
            functools.partial(finish_kernel, sizes[:3], per, width),
            out_shape=shape((outs, cols, rows), f32),
            in_specs=[whole()] * (1 + len(weights) + len(pieces)),
            out_specs=whole(),
            scratch_shapes=[
                pltpu.VMEM((batches * batch, chans, rows), f32),
                pltpu.VMEM((batches * batch, chans, rows), f32),
                pltpu.VMEM((batches * batch, chans, rows), f32),
                pltpu.VMEM((steps * step, chans, rows), half),
                pltpu.VMEM((cols + 1, chans, rows), f32),
                pltpu.VMEM((cols, chans, rows), half),
                pltpu.VMEM((2, TILE, rows), half),
                *(
                    pltpu.VMEM((TILE, rows) if db else (2, chans, rows), half)
                    for dp, db in MOVES
                ),
                pltpu.VMEM((cols + 4, 3 * chans, 2 * rows), half),
                pltpu.VMEM((cols + 2, 3 * chans, 2 * rows), half),
                pltpu.SMEM(tokens.shape, jnp.int32),
                dma,
                dma((len(MOVES),)),
                dma((len(MOVES),)),
            ],
            compiler_params=pltpu.CompilerParams(
                collective_id=identity, has_side_effects=True, vmem_limit_bytes=24 * MIB
            ),
            name="finish",
        )(tokens, *weights, *(ref.reshape(passes * ncols, -1, chans, rows) for ref in pieces))

    def branch(n, more, width):
        def run(tokens, weights, banded, shifts, revisits):
            if not more:
                return finish(width, 1 + 2 * n, tokens, weights, banded)
            rest = pl.pallas_call(
                functools.partial(rest_kernel, sizes, slots),
                out_shape=shape((passes, bands, own_cols, more, chans, rows), half),
                in_specs=[whole(pltpu.HBM)] * 2,
                out_specs=whole(),
                scratch_shapes=[
                    pltpu.VMEM((bands, own_cols, more, chans, rows), half),
                    pltpu.SMEM((2, per), jnp.int32),
                    pltpu.VMEM(revisits.shape, half),
                    dma((2,)),
                    *exchange_sems,
                ],
                compiler_params=pltpu.CompilerParams(
                    collective_id=2 + 2 * n, has_side_effects=True, vmem_limit_bytes=16 * MIB
                ),
                name="rest",
            )(*in_hbm(shifts, revisits))
            return finish(width, 1 + 2 * n, tokens, weights, banded, rest)

        return run

    weights = (gains, t_qkv, t_out, t_in, w_back.T, t_w1, t_w2)
    plans = [(0, width) for width in widths(count)]
    if per > slots:
        plans += [(1, widths(count)[-3]), (1, count), (per - slots, count)]
    branches = [branch(n, *plan) for n, plan in enumerate(plans)]
    result = lax.switch(which[0], branches, tokens, weights, banded, shifts.T, revisits)
    return result.transpose(1, 0, 2)


def solution(mesh):
    shape = mesh.shape
    sizes = (shape["row"], shape["tile"] * shape["row"], shape["pass"], shape["groups"])
    fixed = [P()] * 12
    return jax.shard_map(
        functools.partial(local, sizes),
        mesh=mesh,
        in_specs=(
            P(("groups", "pass"), ("tile", "row"), None, None),
            P(("groups", "pass"), None),
            P("groups", ("tile", "row")),
            *fixed,
        ),
        out_specs=P(("groups", "pass"), None, ("tile", "row")),
        check_vma=False,
    )
```
